32 devices in a mesh: lat: 4 (over y, core), lon: 8 (over z, x).
Axes of the slice: x: 2, y: 2, z: 4, core: 2. Of those that a mesh axis runs over, the one named last changes fastest.
Arguments:
- state: float32 [4, 8, 448, 4096], P(None, None, 'lat', 'lon'), may hold values from -6 to 6
- level_courant: float32 [8], replicated, may hold values from 0.05 to 0.3
- damp_table: float32 [16, 2048], replicated, may hold values from 0.05 to 1
- row_flag: int32 [448], P('lat'), may hold values from 0 to 1, as said below
- row_table: int32 [448], P('lat'), may hold values from 0 to 15
- partner: int32 [4096], P('lon'), may hold values from 0 to 4095, each once
Outputs:
- new_state: float32 [4, 8, 448, 4096], P(None, None, 'lat', 'lon')
The draws below stay inside these ranges and needn't reach their ends.
Inputs may be any that keep to these rules, and one draw needn't show every extreme that they name: `row_flag`: 0 on every row from 112 to 335; each row of the outer quarters is 1 or 0 on its own; the first and the last row are 1. `partner`: a permutation of the columns.
All inputs are finite; a program needn't handle non-finite values.
Results may differ from the reference program's by a relative error of at most 0.00005.
Values sent between devices are 32-bit elements; how exact they have to be, the bound alone decides.
A program may use at most 128 MiB of HBM per device.

```python
import math
import jax
import jax.numpy as jnp
from jax import lax

NLON = 4096
LEVELS = 8
FIELDS = 4
NTAB = 16
NLAT = 448


def draw_row_flag(key, part):
    row_ids = jnp.arange(NLAT, dtype=jnp.int32)
    coins = jax.random.randint(key, (NLAT,), 0, 4, dtype=jnp.int32)
    polar = (row_ids < NLAT // 4) | (row_ids >= NLAT - NLAT // 4)
    ends = (row_ids == 0) | (row_ids == NLAT - 1)
    return (polar & (coins > 0) | ends).astype(jnp.int32)


def touch_ends(values, key, smallest, top_value):
    index_at = [jax.random.randint(jax.random.fold_in(key, axis), (), 0, length) for axis, length in enumerate(values.shape)]
    main_axis = values.shape.index(max(values.shape))
    beside = index_at[:main_axis] + [(index_at[main_axis] + 1) % values.shape[main_axis]] + index_at[main_axis + 1:]
    return values.at[tuple(index_at)].set(smallest).at[tuple(beside)].set(top_value)


def block_scale(rng, shape, split, smallest, top_value):
    loudness, own = 1.0, jax.random.fold_in(rng, 6)
    for dim, shards_of in split:
        steps = jnp.exp(jax.random.uniform(jax.random.fold_in(own, dim), (shards_of,), jnp.float32, smallest / len(split), top_value / len(split)))
        loudness = loudness * jnp.repeat(steps, shape[dim] // shards_of).reshape([-1 if axis == dim else 1 for axis in range(len(shape))])
    return loudness


def centred(rng, shape, deviation, reach, cuts=(), kind=jnp.bfloat16):
    factor_of = block_scale(rng, shape, cuts, -0.22, 0.18) if cuts else 1.0
    values = jax.random.normal(rng, shape, jnp.float32) * deviation * factor_of
    return jnp.minimum(jnp.maximum(values, -reach), reach).astype(kind)


def setup_inputs(seed: int = 0) -> dict:
    streams_of = jax.random.split(jax.random.key(seed), 7)
    return {
        "state": centred(streams_of[0], (FIELDS, LEVELS, NLAT, NLON), 1.0, 6.0, ((2, 4), (3, 8)), jnp.float32),
        "level_courant": jnp.clip(jnp.exp(jax.random.uniform(streams_of[1], (LEVELS,), jnp.float32, math.log(0.05), math.log(0.3))), 0.05, 0.3),
        "damp_table": jnp.clip(jnp.exp(jax.random.uniform(streams_of[2], (NTAB, NLON // 2), jnp.float32, math.log(0.05), math.log(1.0))), 0.05, 1.0),
        "row_flag": draw_row_flag(jax.random.fold_in(streams_of[6], 71), 0),
        "row_table": touch_ends(jax.random.randint(streams_of[4], (NLAT,), 0, NTAB), jax.random.fold_in(streams_of[4], 1), 0, NTAB - 1).astype(jnp.int32),
        "partner": jax.random.permutation(streams_of[5], NLON).astype(jnp.int32),
    }


coriolis = 0.3
cos_floor = 0.25


def neighbours(values, sign, partner):
    eastward = jnp.roll(values, -1, axis=1)
    westward = jnp.roll(values, 1, axis=1)
    top_row = sign * values[-1][partner]
    low_row = sign * values[0][partner]
    northward = jnp.concatenate([values[1:], top_row[None, :]], axis=0)
    southward = jnp.concatenate([low_row[None, :], values[:-1]], axis=0)
    return eastward, westward, northward, southward


def reference(state, level_courant, damp_table, row_flag, row_table, partner):
    row_pos = jnp.arange(NLAT).astype(jnp.float32)
    latitude = -jnp.pi / 2 + jnp.pi * (row_pos + 0.5) / NLAT
    cos_lat = jnp.cos(latitude)[:, None]
    sin_lat = jnp.sin(latitude)[:, None]
    metric = 1.0 / jnp.maximum(cos_lat, cos_floor)
    pick = (row_table[:, None] == jnp.arange(NTAB)[None, :]).astype(jnp.float32)
    half_damp = jnp.dot(pick, damp_table, precision=lax.Precision.HIGHEST, preferred_element_type=jnp.float32)
    damping = jnp.concatenate([jnp.ones((NLAT, 1), jnp.float32), half_damp], axis=1)
    flagged = (row_flag == 1)[None, :, None]

    def one_level(inputs):
        fields, courant = inputs
        pressure, wind_u, wind_v, thermo = fields[0], fields[1], fields[2], fields[3]
        p_east, p_west, p_north, p_south = neighbours(pressure, 1.0, partner)
        t_east, t_west, t_north, t_south = neighbours(thermo, 1.0, partner)
        tend_u = -courant * metric * (p_east - p_west) * 0.5 + coriolis * sin_lat * wind_v
        tend_v = -courant * (p_north - p_south) * 0.5 - coriolis * sin_lat * wind_u
        u_new = wind_u + tend_u
        v_new = wind_v + tend_v
        flux = v_new * cos_lat
        u_east, u_west, _, _ = neighbours(u_new, -1.0, partner)
        _, _, f_north, f_south = neighbours(flux, -1.0, partner)
        divergence = courant * metric * ((u_east - u_west) * 0.5 + (f_north - f_south) * 0.5)
        tend_t = -courant * metric * u_new * (t_east - t_west) * 0.5 - courant * v_new * (t_north - t_south) * 0.5
        increments = jnp.stack([-divergence, tend_u, tend_v, tend_t])
        spectrum = jnp.fft.rfft(increments, axis=-1)
        smoothed = jnp.fft.irfft(spectrum * damping[None], n=NLON, axis=-1).astype(increments.dtype)
        increments = jnp.where(flagged, smoothed, increments)
        return fields + increments

    result = lax.map(one_level, (jnp.transpose(state, (1, 0, 2, 3)), level_courant))
    return jnp.transpose(result, (1, 0, 2, 3))
```

```python
import functools
import math

import jax
import jax.numpy as jnp
import numpy as np
from jax import lax
from jax.experimental import pallas as pl
from jax.experimental.pallas import tpu as pltpu
from jax.sharding import PartitionSpec as P

coriolis = 0.3
cos_floor = 0.25
MESH = pl.DeviceIdType.MESH
OUTER = 32
INNER = 128
HALF = OUTER // 2 + 1


def halo_kernel(rows_ref, cols_ref, rows_out, cols_out, circle_ref, lat_send, lat_recv, lon_send, lon_recv, cir_send, cir_recv):
    a, j = lax.axis_index("lat"), lax.axis_index("lon")
    na, nj = lax.axis_size("lat"), lax.axis_size("lon")
    barrier = pltpu.get_barrier_semaphore()

    def greet(t, carry):
        pl.semaphore_signal(barrier, inc=1, device_id=(a, lax.rem(j + t, nj)), device_id_type=MESH)
        return carry

    lax.fori_loop(1, nj, greet, 0)

    for near in (lax.rem(a + 1, na), lax.rem(a + na - 1, na)):
        pl.semaphore_signal(barrier, inc=1, device_id=(near, j), device_id_type=MESH)
    pl.semaphore_wait(barrier, nj + 1)

    pole = jnp.logical_or(a == 0, a == na - 1)
    side = jnp.where(a == 0, 0, 1)

    def lat_copy(s):
        target = a - 1 if s == 0 else a + 1
        return pltpu.make_async_remote_copy(
            rows_ref.at[s], rows_out.at[1 - s], lat_send.at[s], lat_recv.at[1 - s],
            device_id=(target, j), device_id_type=MESH)

    def lon_copy(s):
        target = lax.rem(j + (nj - 1 if s == 0 else 1), nj)
        return pltpu.make_async_remote_copy(
            cols_ref.at[s], cols_out.at[1 - s], lon_send.at[s], lon_recv.at[1 - s],
            device_id=(a, target), device_id_type=MESH)

    def circle_copy(t):
        return pltpu.make_async_remote_copy(
            rows_ref.at[side], circle_ref.at[j], cir_send.at[t], cir_recv.at[j],
            device_id=(a, lax.rem(j + t, nj)), device_id_type=MESH)

    def circle_wait(t):
        source = lax.rem(j + t, nj)
        return pltpu.make_async_remote_copy(
            rows_ref.at[side], circle_ref.at[source], cir_send.at[t], cir_recv.at[source],
            device_id=(a, source), device_id_type=MESH)

    own = pltpu.make_async_copy(rows_ref.at[side], circle_ref.at[j], cir_recv.at[j])

    @pl.when(pole)
    def _():
        lax.fori_loop(1, nj, lambda t, c: (circle_copy(t).start(), c)[1], 0)
        own.start()

    lon_copy(0).start()
    lon_copy(1).start()

    @pl.when(a > 0)
    def _():
        lat_copy(0).start()

    @pl.when(a < na - 1)
    def _():
        lat_copy(1).start()

    lon_copy(0).wait()
    lon_copy(1).wait()

    @pl.when(a > 0)
    def _():
        lat_copy(0).wait_send()
        lat_copy(1).wait_recv()

    @pl.when(a < na - 1)
    def _():
        lat_copy(1).wait_send()
        lat_copy(0).wait_recv()

    @pl.when(pole)
    def _():
        def finish(t, carry):
            circle_copy(t).wait_send()
            circle_wait(t).wait_recv()
            return carry

        lax.fori_loop(1, nj, finish, 0)
        own.wait()


def exchange_halos(rows, cols):
    nj = lax.axis_size("lon")
    vmem = pl.BlockSpec(memory_space=pltpu.VMEM)
    dma = pltpu.SemaphoreType.DMA
    return pl.pallas_call(
        halo_kernel,
        out_shape=(
            jax.ShapeDtypeStruct(rows.shape, jnp.float32),
            jax.ShapeDtypeStruct(cols.shape, jnp.float32),
            jax.ShapeDtypeStruct((nj,) + rows.shape[1:], jnp.float32),
        ),
        in_specs=[vmem, vmem],
        out_specs=(vmem, vmem, vmem),
        scratch_shapes=[dma((2,)), dma((2,)), dma((2,)), dma((2,)), dma((nj,)), dma((nj,))],
        compiler_params=pltpu.CompilerParams(collective_id=0, has_side_effects=True),
        name="halos",
    )(rows, cols)


def real_forward(values):
    n = len(values)
    if n == 1:
        return [(values[0], None)]
    if n == 2:
        return [(values[0] + values[1], None), (values[0] - values[1], None)]
    even = real_forward(values[0::2])
    odd = real_forward(values[1::2])
    half = n // 2
    out = [None] * (half + 1)
    for k in range(half // 2 + 1):
        er, ei = even[k]
        orr, oi = odd[k]
        if k == 0:
            out[0] = (er + orr, None)
            out[half] = (er - orr, None)
            continue
        c, s = math.cos(2 * math.pi * k / n), math.sin(2 * math.pi * k / n)
        if k == half // 2:
            out[k] = (er, -orr)
            continue
        if oi is None:
            tr, ti = c * orr, -s * orr
        else:
            tr, ti = c * orr + s * oi, c * oi - s * orr
        eii = 0.0 if ei is None else ei
        out[k] = (er + tr, eii + ti)
        out[half - k] = (er - tr, ti - eii)
    return out


def real_backward(spec):
    n = 2 * (len(spec) - 1)
    if n == 2:
        return [spec[0][0] + spec[1][0], spec[0][0] - spec[1][0]]
    half = n // 2
    even, odd = [], []
    for k in range(half // 2 + 1):
        xr, xi = spec[k]
        yr, yi = spec[half - k]
        if k == 0:
            even.append((xr + yr, None))
            odd.append((xr - yr, None))
            continue
        if k == half // 2:
            even.append((2.0 * xr, None))
            odd.append((-2.0 * xi, None))
            continue
        c, s = math.cos(2 * math.pi * k / n), math.sin(2 * math.pi * k / n)
        dr, di = xr - yr, xi + yi
        even.append((xr + yr, xi - yi))
        odd.append((c * dr - s * di, c * di + s * dr))
    out = [None] * n
    out[0::2] = real_backward(even)
    out[1::2] = real_backward(odd)
    return out


def split(x):
    high = x.astype(jnp.bfloat16)
    return high, (x - high.astype(jnp.float32)).astype(jnp.bfloat16)


def dot3(x, w_ref):
    high, low = split(x)
    dot = functools.partial(jnp.dot, preferred_element_type=jnp.float32)
    return dot(high, w_ref[0]) + (dot(low, w_ref[0]) + dot(high, w_ref[1]))


def circle_kernel(upd, parts, inc_ref, damp_ref, twid_ref, fwd_ref, bwd_ref, out_ref, recv, done, spec, send1, recv1, send2, recv2):
    a, j = lax.axis_index("lat"), lax.axis_index("lon")
    na, nj = lax.axis_size("lat"), lax.axis_size("lon")
    quarter = na // 4
    low = a < na // 2
    active = jnp.logical_or(a < quarter, a >= na - quarter)
    mirror = jnp.where(low, 2 * quarter - 1 - a, 2 * na - 2 * quarter - 1 - a)
    source_lat = jnp.where(active, a, mirror)
    helper_lat = jnp.where(active, mirror, a)
    mine = jnp.where(active, j, nj + j)
    count = 2 * nj
    part_rows = recv.shape[2]
    width = recv.shape[3]

    def place(d):
        return (jnp.where(d < nj, source_lat, helper_lat), lax.rem(d, nj))

    def unit(ref, d, c):
        u = d * upd + c
        r = pl.multiple_of(lax.rem(u, parts) * part_rows, 8)
        return ref.at[u // parts, pl.ds(r, part_rows), :]

    barrier = pltpu.get_barrier_semaphore()

    def greet(t, carry):
        pl.semaphore_signal(barrier, inc=1, device_id=place(lax.rem(mine + t, count)), device_id_type=MESH)
        return carry

    lax.fori_loop(1, count, greet, 0)
    pl.semaphore_wait(barrier, count - 1)

    def out_copy(c, t):
        d = lax.rem(mine + t, count)
        return pltpu.make_async_remote_copy(
            unit(inc_ref, d, c), recv.at[c, j], send1.at[c, t], recv1.at[c, j],
            device_id=place(d), device_id_type=MESH)

    def out_own(c):
        return pltpu.make_async_copy(unit(inc_ref, mine, c), recv.at[c, j], recv1.at[c, j])

    def in_wait(c, s):
        return pltpu.make_async_remote_copy(
            unit(inc_ref, mine, c), recv.at[c, s], send1.at[c, 0], recv1.at[c, s],
            device_id=(source_lat, s), device_id_type=MESH)

    def back_copy(c, s):
        return pltpu.make_async_remote_copy(
            done.at[c, s], unit(out_ref, mine, c), send2.at[c, s], recv2.at[c, mine],
            device_id=(source_lat, s), device_id_type=MESH)

    def back_own(c):
        return pltpu.make_async_copy(done.at[c, j], unit(out_ref, mine, c), recv2.at[c, mine])

    def back_wait(c, d):
        return pltpu.make_async_remote_copy(
            done.at[c, j], unit(out_ref, d, c), send2.at[c, j], recv2.at[c, d],
            device_id=place(d), device_id_type=MESH)

    @pl.when(active)
    def _():
        def launch(c, carry):
            lax.fori_loop(1, count, lambda t, k: (out_copy(c, t).start(), k)[1], 0)
            out_own(c).start()
            return carry

        lax.fori_loop(0, upd, launch, 0)

    tiles = part_rows // 8
    per = width // INNER

    def handle(c, carry):
        def arrive(t, k):
            in_wait(c, lax.rem(j + t, nj)).wait_recv()
            return k

        lax.fori_loop(1, nj, arrive, 0)

        @pl.when(active)
        def _():
            out_own(c).wait()

        @pl.when(jnp.logical_not(active))
        def _():
            in_wait(c, j).wait_recv()

        def analyse(i, k):
            r = pl.ds(pl.multiple_of(i * 8, 8), 8)
            values = [
                recv[c, p // per, r, (p % per) * INNER : (p % per + 1) * INNER] for p in range(OUTER)
            ]
            for q, (re, im) in enumerate(real_forward(values)):
                cos, sin = twid_ref[0, q : q + 1, :], twid_ref[1, q : q + 1, :]
                if im is None:
                    spec[q, r, :INNER] = re * cos
                    spec[q, r, INNER:] = -re * sin
                else:
                    spec[q, r, :INNER] = re * cos + im * sin
                    spec[q, r, INNER:] = im * cos - re * sin
            return k

        lax.fori_loop(0, tiles, analyse, 0)
        h = lax.rem(mine * upd + c, parts)
        full = dot3(spec[...].reshape(HALF * part_rows, 2 * INNER), fwd_ref)
        weight = damp_ref[h].reshape(HALF * part_rows, INNER)
        full = full * jnp.concatenate([weight, weight], axis=1)
        spec[...] = dot3(full, bwd_ref).reshape(HALF, part_rows, 2 * INNER)

        def synthesise(i, k):
            r = pl.ds(pl.multiple_of(i * 8, 8), 8)
            waves = []
            for q in range(HALF):
                cos, sin = twid_ref[0, q : q + 1, :], twid_ref[1, q : q + 1, :]
                re, im = spec[q, r, :INNER], spec[q, r, INNER:]
                waves.append((re * cos - im * sin, im * cos + re * sin))
            for p, value in enumerate(real_backward(waves)):
                done[c, p // per, r, (p % per) * INNER : (p % per + 1) * INNER] = value
            return k

        lax.fori_loop(0, tiles, synthesise, 0)
        lax.fori_loop(1, nj, lambda t, k: (back_copy(c, lax.rem(j + t, nj)).start(), k)[1], 0)

        @pl.when(active)
        def _():
            back_own(c).start()

        @pl.when(jnp.logical_not(active))
        def _():
            back_copy(c, j).start()

        return carry

    lax.fori_loop(0, upd, handle, 0)

    def settle(c, carry):
        lax.fori_loop(1, nj, lambda t, k: (back_copy(c, lax.rem(j + t, nj)).wait_send(), k)[1], 0)

        @pl.when(active)
        def _():
            def finish(t, k):
                out_copy(c, t).wait_send()
                back_wait(c, lax.rem(mine + t, count)).wait_recv()
                return k

            lax.fori_loop(1, count, finish, 0)
            back_own(c).wait()

        @pl.when(jnp.logical_not(active))
        def _():
            back_copy(c, j).wait_send()

        return carry

    lax.fori_loop(0, upd, settle, 0)


def constants():
    k = np.arange(HALF)[:, None]
    q = np.arange(INNER)[None, :]
    turn = 2 * np.pi * (k * q) / (OUTER * INNER)
    twiddle = np.stack([np.cos(turn), np.sin(turn)]).astype(np.float32)
    turn = 2 * np.pi * ((q.T * q) % INNER) / INNER
    cos, sin = np.cos(turn), np.sin(turn)
    forward = np.block([[cos, -sin], [sin, cos]])

    def pair(m):
        high = m.astype(jnp.bfloat16)
        return np.stack([high, (m - high.astype(np.float64)).astype(jnp.bfloat16)])

    return jnp.asarray(twiddle), jnp.asarray(pair(forward)), jnp.asarray(pair(forward.T))


def filter_circles(inc, weights, parts):
    nj = lax.axis_size("lon")
    stacks, rows, width = inc.shape
    upd = stacks * parts // (2 * nj)
    part_rows = rows // parts
    vmem = pl.BlockSpec(memory_space=pltpu.VMEM)
    hbm = pl.BlockSpec(memory_space=pl.ANY)
    dma = pltpu.SemaphoreType.DMA
    twiddle, forward, backward = constants()
    return pl.pallas_call(
        functools.partial(circle_kernel, upd, parts),
        out_shape=jax.ShapeDtypeStruct(inc.shape, jnp.float32),
        in_specs=[hbm, vmem, vmem, vmem, vmem],
        out_specs=hbm,
        scratch_shapes=[
            pltpu.VMEM((upd, nj, part_rows, width), jnp.float32),
            pltpu.VMEM((upd, nj, part_rows, width), jnp.float32),
            pltpu.VMEM((HALF, part_rows, 2 * INNER), jnp.float32),
            dma((upd, 2 * nj)),
            dma((upd, nj)),
            dma((upd, nj)),
            dma((upd, 2 * nj)),
        ],
        compiler_params=pltpu.CompilerParams(
            collective_id=1, has_side_effects=True, vmem_limit_bytes=40 * 1024 * 1024
        ),
        name="circles",
    )(inc, weights, twiddle, forward, backward)


def per_device(state, level_courant, damp_table, row_flag, row_table, partner):
    fields_n, levels_n, rows_n, cols_n = state.shape
    na = lax.axis_size("lat")
    a = lax.axis_index("lat")
    whole_rows = rows_n * na

    def geometry(row_pos):
        latitude = -jnp.pi / 2 + jnp.pi * (row_pos.astype(jnp.float32) + 0.5) / whole_rows
        return jnp.cos(latitude), jnp.sin(latitude)

    first_row = a * rows_n
    cos1, sin1 = geometry(first_row + jnp.arange(rows_n, dtype=jnp.int32))
    cos_lat, sin_lat = cos1[:, None], sin1[:, None]
    metric1 = 1.0 / jnp.maximum(cos1, cos_floor)
    metric = metric1[:, None]
    c1 = level_courant[:, None]
    courant = level_courant[:, None, None]
    p, u, v, th = state[0], state[1], state[2], state[3]
    meet = jnp.broadcast_to(partner.astype(jnp.float32)[None, :], (8, cols_n))

    def row_pack(outer, inner):
        return jnp.concatenate(
            [p[:, outer], p[:, inner], u[:, outer], v[:, outer], th[:, outer], meet], axis=0
        )

    def col_pack(outer, inner):
        return jnp.concatenate(
            [p[:, :, outer], p[:, :, inner], u[:, :, outer], v[:, :, outer], th[:, :, outer]], axis=0
        )

    rows = jnp.stack([row_pack(0, 1), row_pack(rows_n - 1, rows_n - 2)])
    cols = jnp.stack([col_pack(0, 1), col_pack(cols_n - 1, cols_n - 2)])
    rows_in, cols_in, circle = exchange_halos(rows, cols)

    def fields_of(pack):
        return [pack[8 * k : 8 * k + 8] for k in range(5)]

    at_south, at_north = a == 0, a == na - 1
    whole = jnp.transpose(circle, (1, 0, 2)).reshape(circle.shape[1], -1)
    met = jnp.take(whole, partner, axis=1)
    twice = jnp.clip(met[40].astype(jnp.int32), 0, whole.shape[1] - 1)
    p_twice = jnp.take(whole[:8], twice, axis=1)
    p_met, p_met_in, u_met, v_met, th_met = fields_of(met)
    cos_end = jnp.where(at_south, cos1[0], cos1[-1])
    sin_end = jnp.where(at_south, sin1[0], sin1[-1])
    rise = jnp.where(at_south, p_met_in - p_twice, p_twice - p_met_in)
    flux_met = -(v_met + (-c1 * rise * 0.5 - coriolis * sin_end * u_met)) * cos_end

    ps, ps2, us, vs, ths = fields_of(rows_in[0])
    pn, pn2, un, vn, thn = fields_of(rows_in[1])
    cos_s, sin_s = geometry(first_row - 1)
    cos_n, sin_n = geometry(first_row + rows_n)
    flux_s = (vs + (-c1 * (p[:, 0] - ps2) * 0.5 - coriolis * sin_s * us)) * cos_s
    flux_n = (vn + (-c1 * (pn2 - p[:, -1]) * 0.5 - coriolis * sin_n * un)) * cos_n
    ps, ths, flux_s = (jnp.where(at_south, m, o) for m, o in ((p_met, ps), (th_met, ths), (flux_met, flux_s)))
    pn, thn, flux_n = (jnp.where(at_north, m, o) for m, o in ((p_met, pn), (th_met, thn), (flux_met, flux_n)))

    pw, pw2, uw, vw, thw = fields_of(cols_in[0])
    pe, pe2, ue, ve, the = fields_of(cols_in[1])
    u_west = uw + (-c1 * metric1 * (p[:, :, 0] - pw2) * 0.5 + coriolis * sin1 * vw)
    u_east = ue + (-c1 * metric1 * (pe2 - p[:, :, -1]) * 0.5 + coriolis * sin1 * ve)

    def zonal(f, west, east):
        return jnp.concatenate([f[:, :, 1:], east[:, :, None]], axis=2) - jnp.concatenate(
            [west[:, :, None], f[:, :, :-1]], axis=2
        )

    def merid(f, south, north):
        return jnp.concatenate([f[:, 1:], north[:, None, :]], axis=1) - jnp.concatenate(
            [south[:, None, :], f[:, :-1]], axis=1
        )

    tend_u = -courant * metric * zonal(p, pw, pe) * 0.5 + coriolis * sin_lat * v
    tend_v = -courant * merid(p, ps, pn) * 0.5 - coriolis * sin_lat * u
    u_new = u + tend_u
    v_new = v + tend_v
    flux = v_new * cos_lat
    divergence = courant * metric * (zonal(u_new, u_west, u_east) * 0.5 + merid(flux, flux_s, flux_n) * 0.5)
    tend_t = -courant * metric * u_new * zonal(th, thw, the) * 0.5 - courant * v_new * merid(th, ths, thn) * 0.5
    inc = jnp.concatenate([-divergence, tend_u, tend_v, tend_t])

    quarter = na // 4
    pairs = [(i, 2 * quarter - 1 - i if i < na // 2 else 2 * na - 2 * quarter - 1 - i) for i in range(na)]
    active = (a < quarter) | (a >= na - quarter)
    table = jnp.where(active, row_table, lax.ppermute(row_table, "lat", pairs))
    parts = 2
    count = damp_table.shape[0]
    length = OUTER * INNER
    full = jnp.concatenate(
        [jnp.ones((count, 1), jnp.float32), damp_table, jnp.flip(damp_table[:, :-1], axis=1)], axis=1
    )
    grid = jnp.transpose(full.reshape(count, INNER, OUTER), (0, 2, 1))[:, :HALF] * (1.0 / length)
    pick = (table[:, None] == jnp.arange(count, dtype=jnp.int32)[None, :]).astype(jnp.float32)
    weights = jnp.einsum(
        "hrt,tkm->hkrm", pick.reshape(parts, rows_n // parts, count), grid, precision=lax.Precision.HIGHEST
    )
    smooth = filter_circles(inc, weights, parts)
    chosen = (active & (row_flag == 1))[None, :, None]
    result = state.reshape(inc.shape) + jnp.where(chosen, smooth, inc)
    return result.reshape(state.shape)


def solution(mesh):
    placed = (P(None, None, "lat", "lon"), P(), P(), P("lat"), P("lat"), P("lon"))
    return jax.shard_map(
        per_device,
        mesh=mesh,
        in_specs=placed,
        out_specs=P(None, None, "lat", "lon"),
        check_vma=False,
    )
```

```python
import functools
import math

import jax
import jax.numpy as jnp
import numpy as np
from jax import lax
from jax.experimental import pallas as pl
from jax.experimental.pallas import tpu as pltpu
from jax.sharding import PartitionSpec as P

coriolis = 0.3
cos_floor = 0.25
MESH = pl.DeviceIdType.MESH
OUTER = 32
INNER = 128
HALF = OUTER // 2 + 1


def wide(tile, width):
    count = width // INNER
    return tile if count == 1 else jnp.concatenate([tile] * count, axis=1)


def step_kernel(
    c_ref, ends_ref, state_ref, geo_ref, ccol_ref, clane_ref, meet_ref, inc_ref,
    rows, cols, rows_in, cols_in, circle, eff, edge, side_cols, pad_p, pad_t, pad_f,
    lat_send, lat_recv, lon_send, lon_recv, cir_send, cir_recv,
):
    a, j = lax.axis_index("lat"), lax.axis_index("lon")
    na, nj = lax.axis_size("lat"), lax.axis_size("lon")
    levels, height, width = state_ref.shape[1:]
    barrier = pltpu.get_barrier_semaphore()

    def greet(t, carry):
        pl.semaphore_signal(barrier, inc=1, device_id=(a, lax.rem(j + t, nj)), device_id_type=MESH)
        return carry

    lax.fori_loop(1, nj, greet, 0)
    for near in (lax.rem(a + 1, na), lax.rem(a + na - 1, na)):
        pl.semaphore_signal(barrier, inc=1, device_id=(near, j), device_id_type=MESH)

    order = (0, 0, 1, 2, 3)
    for s in range(2):
        for k, f in enumerate(order):
            inner = 1 if k == 1 else 0
            r = inner if s == 0 else height - 1 - inner
            for l in range(levels):
                rows[s, 8 * k + l : 8 * k + l + 1, :] = state_ref[f, l, r : r + 1, :]
        rows[s, 40:48, :] = meet_ref[...]
    lane = lax.broadcasted_iota(jnp.int32, (height, INNER), 1)
    for s in range(2):
        packed = jnp.zeros((height, INNER), jnp.float32)
        for k, f in enumerate(order):
            inner = 1 if k == 1 else 0
            source = inner if s == 0 else INNER - 1 - inner
            start = 0 if s == 0 else width - INNER
            for l in range(levels):
                tile = state_ref[f, l, :, start : start + INNER]
                spot = 8 * k + l
                shift = (spot - source) % INNER
                if shift:
                    tile = pltpu.roll(tile, shift, 1)
                packed = jnp.where(lane == spot, tile, packed)
        cols[s] = packed
    pl.semaphore_wait(barrier, nj + 1)

    pole = jnp.logical_or(a == 0, a == na - 1)
    side = jnp.where(a == 0, 0, 1)

    def lat_copy(s):
        target = a - 1 if s == 0 else a + 1
        return pltpu.make_async_remote_copy(
            rows.at[s], rows_in.at[1 - s], lat_send.at[s], lat_recv.at[1 - s],
            device_id=(target, j), device_id_type=MESH)

    def lon_copy(s):
        target = lax.rem(j + (nj - 1 if s == 0 else 1), nj)
        return pltpu.make_async_remote_copy(
            cols.at[s], cols_in.at[1 - s], lon_send.at[s], lon_recv.at[1 - s],
            device_id=(a, target), device_id_type=MESH)

    def circle_copy(t):
        return pltpu.make_async_remote_copy(
            rows.at[side], circle.at[j], cir_send.at[t], cir_recv.at[j],
            device_id=(a, lax.rem(j + t, nj)), device_id_type=MESH)

    def circle_wait(t):
        source = lax.rem(j + t, nj)
        return pltpu.make_async_remote_copy(
            rows.at[side], circle.at[source], cir_send.at[t], cir_recv.at[source],
            device_id=(a, source), device_id_type=MESH)

    own = pltpu.make_async_copy(rows.at[side], circle.at[j], cir_recv.at[j])

    @pl.when(pole)
    def _():
        lax.fori_loop(1, nj, lambda t, c: (circle_copy(t).start(), c)[1], 0)
        own.start()

    @pl.when(a > 0)
    def _():
        lat_copy(0).start()

    @pl.when(a < na - 1)
    def _():
        lat_copy(1).start()

    lon_copy(0).start()
    lon_copy(1).start()

    @pl.when(a > 0)
    def _():
        lat_copy(0).wait_send()
        lat_copy(1).wait_recv()

    @pl.when(a < na - 1)
    def _():
        lat_copy(1).wait_send()
        lat_copy(0).wait_recv()

    ccol = wide(ccol_ref[...], width)

    for s in range(2):
        near, far, u, v, th = (rows_in[s, 8 * k : 8 * k + 8, :] for k in range(5))
        first = rows[s, 0:8, :]
        rise = first - far if s == 0 else far - first
        flux = (v + (-ccol * rise * 0.5 - coriolis * ends_ref[2 * s + 1] * u)) * ends_ref[2 * s]
        eff[s, 0:8, :] = near
        eff[s, 8:16, :] = th
        eff[s, 16:24, :] = flux

    @pl.when(pole)
    def _():
        def finish(t, carry):
            circle_copy(t).wait_send()
            circle_wait(t).wait_recv()
            return carry

        lax.fori_loop(1, nj, finish, 0)
        own.wait()
        column = lax.broadcasted_iota(jnp.int32, (width, width), 0)

        def gather(count, where):
            def add(s, total):
                x = circle[s, 0:count, :]
                high = x.astype(jnp.bfloat16).astype(jnp.float32)
                rest = x - high
                middle = rest.astype(jnp.bfloat16).astype(jnp.float32)
                pieces = jnp.concatenate([high, middle, rest - middle], axis=0).astype(jnp.bfloat16)
                hit = (column + s * width).astype(jnp.float32) == where
                chosen = jnp.where(hit, 1.0, 0.0).astype(jnp.bfloat16)
                return total + jnp.dot(pieces, chosen, preferred_element_type=jnp.float32)

            total = lax.fori_loop(0, nj, add, jnp.zeros((3 * count, width), jnp.float32))
            return (total[:count] + total[count : 2 * count]) + total[2 * count :]

        met = gather(48, meet_ref[0:1, :])
        twice = gather(8, met[40:41])
        near, inner, u, v, th = (met[8 * k : 8 * k + 8] for k in range(5))
        rise = jnp.where(a == 0, 1.0, -1.0) * (inner - twice)
        flux = -(v + (-ccol * rise * 0.5 - coriolis * ends_ref[5] * u)) * ends_ref[4]
        eff[side, 0:8, :] = near
        eff[side, 8:16, :] = th
        eff[side, 16:24, :] = flux

    lon_copy(0).wait()
    lon_copy(1).wait()

    for s in range(2):
        got = cols_in[s]
        first = cols[s]
        far, u, v = (pltpu.roll(got, INNER - 8 * k, 1) for k in (1, 2, 3))
        rise = first - far if s == 0 else far - first
        fresh = u + (-clane_ref[0:1, :] * geo_ref[2] * rise * 0.5 + coriolis * geo_ref[1] * v)
        edge[s] = jnp.where(lane < 40, got, pltpu.roll(fresh, 40, 1))

    lanes = lax.broadcasted_iota(jnp.int32, (8, width), 1)

    def level(l, carry):
        c = c_ref[l]
        for k, lane0 in enumerate((0, 32, 40)):
            side_cols[2 * k] = pltpu.roll(edge[0], INNER - lane0 - l, 1)
            side_cols[2 * k + 1] = pltpu.roll(edge[1], INNER - 1 - lane0 - l, 1)
        inside = slice(8, 8 + height)
        pad_p[inside, :] = state_ref[0, l]
        pad_t[inside, :] = state_ref[3, l]
        for k, pad in enumerate((pad_p, pad_t, pad_f)):
            pad[7:8, :] = eff[0, pl.ds(8 * k + l, 1), :]
            pad[8 + height : 9 + height, :] = eff[1, pl.ds(8 * k + l, 1), :]

        def zonal(x, k, r):
            west = jnp.where(lanes == 0, wide(side_cols[2 * k, r, :], width), pltpu.roll(x, 1, 1))
            east = jnp.where(
                lanes == width - 1, wide(side_cols[2 * k + 1, r, :], width), pltpu.roll(x, width - 1, 1)
            )
            return east - west

        def merid(pad, i):
            return pad[9 + 8 * i : 17 + 8 * i, :] - pad[7 + 8 * i : 15 + 8 * i, :]

        for i in range(height // 8):
            r = slice(8 * i, 8 * i + 8)
            cos, sin, metric = (wide(geo_ref[k, r, :], width) for k in range(3))
            u, v = state_ref[1, l, r, :], state_ref[2, l, r, :]
            tend_u = -c * metric * zonal(state_ref[0, l, r, :], 0, r) * 0.5 + coriolis * sin * v
            tend_v = -c * merid(pad_p, i) * 0.5 - coriolis * sin * u
            u_new, v_new = u + tend_u, v + tend_v
            pad_f[8 + 8 * i : 16 + 8 * i, :] = v_new * cos
            inc_ref[levels + l, r, :] = tend_u
            inc_ref[2 * levels + l, r, :] = tend_v
            inc_ref[3 * levels + l, r, :] = (
                -c * metric * u_new * zonal(state_ref[3, l, r, :], 1, r) * 0.5 - c * v_new * merid(pad_t, i) * 0.5
            )
            inc_ref[l, r, :] = zonal(u_new, 2, r) * 0.5
        for i in range(height // 8):
            r = slice(8 * i, 8 * i + 8)
            metric = wide(geo_ref[2, r, :], width)
            inc_ref[l, r, :] = -(c * metric * (inc_ref[l, r, :] + merid(pad_f, i) * 0.5))
        return carry

    lax.fori_loop(0, levels, level, 0)


def increments_of(state, level_courant, partner, geo, ends):
    fields, levels, height, width = state.shape
    nj = lax.axis_size("lon")
    vmem = pl.BlockSpec(memory_space=pltpu.VMEM)
    smem = pl.BlockSpec(memory_space=pltpu.SMEM)
    dma = pltpu.SemaphoreType.DMA
    f32 = jnp.float32
    ccol = jnp.broadcast_to(level_courant[:, None], (levels, INNER))
    clane = jnp.broadcast_to(jnp.pad(level_courant, (0, INNER - levels))[None], (8, INNER))
    meet = jnp.broadcast_to(partner.astype(f32)[None], (8, width))
    return pl.pallas_call(
        step_kernel,
        out_shape=jax.ShapeDtypeStruct((fields * levels, height, width), f32),
        in_specs=[smem, smem, vmem, vmem, vmem, vmem, vmem],
        out_specs=vmem,
        scratch_shapes=[
            pltpu.VMEM((2, 48, width), f32),
            pltpu.VMEM((2, height, INNER), f32),
            pltpu.VMEM((2, 48, width), f32),
            pltpu.VMEM((2, height, INNER), f32),
            pltpu.VMEM((nj, 48, width), f32),
            pltpu.VMEM((2, 24, width), f32),
            pltpu.VMEM((2, height, INNER), f32),
            pltpu.VMEM((6, height, INNER), f32),
            pltpu.VMEM((height + 16, width), f32),
            pltpu.VMEM((height + 16, width), f32),
            pltpu.VMEM((height + 16, width), f32),
            dma((2,)), dma((2,)), dma((2,)), dma((2,)), dma((nj,)), dma((nj,)),
        ],
        compiler_params=pltpu.CompilerParams(
            collective_id=0, has_side_effects=True, vmem_limit_bytes=40 * 1024 * 1024
        ),
        name="step",
    )(level_courant, ends, state, geo, ccol, clane, meet)


def real_forward(values):
    n = len(values)
    if n == 1:
        return [(values[0], None)]
    if n == 2:
        return [(values[0] + values[1], None), (values[0] - values[1], None)]
    even = real_forward(values[0::2])
    odd = real_forward(values[1::2])
    half = n // 2
    out = [None] * (half + 1)
    for k in range(half // 2 + 1):
        er, ei = even[k]
        orr, oi = odd[k]
        if k == 0:
            out[0] = (er + orr, None)
            out[half] = (er - orr, None)
            continue
        c, s = math.cos(2 * math.pi * k / n), math.sin(2 * math.pi * k / n)
        if k == half // 2:
            out[k] = (er, -orr)
            continue
        if oi is None:
            tr, ti = c * orr, -s * orr
        else:
            tr, ti = c * orr + s * oi, c * oi - s * orr
        eii = 0.0 if ei is None else ei
        out[k] = (er + tr, eii + ti)
        out[half - k] = (er - tr, ti - eii)
    return out


def real_backward(spec):
    n = 2 * (len(spec) - 1)
    if n == 2:
        return [spec[0][0] + spec[1][0], spec[0][0] - spec[1][0]]
    half = n // 2
    even, odd = [], []
    for k in range(half // 2 + 1):
        xr, xi = spec[k]
        yr, yi = spec[half - k]
        if k == 0:
            even.append((xr + yr, None))
            odd.append((xr - yr, None))
            continue
        if k == half // 2:
            even.append((2.0 * xr, None))
            odd.append((-2.0 * xi, None))
            continue
        c, s = math.cos(2 * math.pi * k / n), math.sin(2 * math.pi * k / n)
        dr, di = xr - yr, xi + yi
        even.append((xr + yr, xi - yi))
        odd.append((c * dr - s * di, c * di + s * dr))
    out = [None] * n
    out[0::2] = real_backward(even)
    out[1::2] = real_backward(odd)
    return out


def split(x):
    high = x.astype(jnp.bfloat16)
    return high, (x - high.astype(jnp.float32)).astype(jnp.bfloat16)


def dot3(x, w_ref):
    high, low = split(x)
    dot = functools.partial(jnp.dot, preferred_element_type=jnp.float32)
    return dot(high, w_ref[0]) + (dot(low, w_ref[0]) + dot(high, w_ref[1]))


def circle_kernel(upd, parts, inc_ref, damp_ref, twid_ref, fwd_ref, bwd_ref, out_ref, recv, done, spec, send1, recv1, send2, recv2):
    a, j = lax.axis_index("lat"), lax.axis_index("lon")
    na, nj = lax.axis_size("lat"), lax.axis_size("lon")
    quarter = na // 4
    low = a < na // 2
    active = jnp.logical_or(a < quarter, a >= na - quarter)
    mirror = jnp.where(low, 2 * quarter - 1 - a, 2 * na - 2 * quarter - 1 - a)
    source_lat = jnp.where(active, a, mirror)
    helper_lat = jnp.where(active, mirror, a)
    mine = jnp.where(active, j, nj + j)
    count = 2 * nj
    part_rows = recv.shape[2]
    width = recv.shape[3]

    def place(d):
        return (jnp.where(d < nj, source_lat, helper_lat), lax.rem(d, nj))

    def unit(ref, d, c):
        u = d * upd + c
        r = pl.multiple_of(lax.rem(u, parts) * part_rows, 8)
        return ref.at[u // parts, pl.ds(r, part_rows), :]

    barrier = pltpu.get_barrier_semaphore()

    def greet(t, carry):
        pl.semaphore_signal(barrier, inc=1, device_id=place(lax.rem(mine + t, count)), device_id_type=MESH)
        return carry

    lax.fori_loop(1, count, greet, 0)
    pl.semaphore_wait(barrier, count - 1)

    def out_copy(c, t):
        d = lax.rem(mine + t, count)
        return pltpu.make_async_remote_copy(
            unit(inc_ref, d, c), recv.at[c, j], send1.at[c, t], recv1.at[c, j],
            device_id=place(d), device_id_type=MESH)

    def out_own(c):
        return pltpu.make_async_copy(unit(inc_ref, mine, c), recv.at[c, j], recv1.at[c, j])

    def in_wait(c, s):
        return pltpu.make_async_remote_copy(
            unit(inc_ref, mine, c), recv.at[c, s], send1.at[c, 0], recv1.at[c, s],
            device_id=(source_lat, s), device_id_type=MESH)

    def back_copy(c, s):
        return pltpu.make_async_remote_copy(
            done.at[c, s], unit(out_ref, mine, c), send2.at[c, s], recv2.at[c, mine],
            device_id=(source_lat, s), device_id_type=MESH)

    def back_own(c):
        return pltpu.make_async_copy(done.at[c, j], unit(out_ref, mine, c), recv2.at[c, mine])

    def back_wait(c, d):
        return pltpu.make_async_remote_copy(
            done.at[c, j], unit(out_ref, d, c), send2.at[c, j], recv2.at[c, d],
            device_id=place(d), device_id_type=MESH)

    @pl.when(active)
    def _():
        def launch(c, carry):
            lax.fori_loop(1, count, lambda t, k: (out_copy(c, t).start(), k)[1], 0)
            out_own(c).start()
            return carry

        lax.fori_loop(0, upd, launch, 0)

    tiles = part_rows // 8
    per = width // INNER

    def handle(c, carry):
        def arrive(t, k):
            in_wait(c, lax.rem(j + t, nj)).wait_recv()
            return k

        lax.fori_loop(1, nj, arrive, 0)

        @pl.when(active)
        def _():
            out_own(c).wait()

        @pl.when(jnp.logical_not(active))
        def _():
            in_wait(c, j).wait_recv()

        def analyse(i, k):
            r = pl.ds(pl.multiple_of(i * 8, 8), 8)
            values = [
                recv[c, p // per, r, (p % per) * INNER : (p % per + 1) * INNER] for p in range(OUTER)
            ]
            for q, (re, im) in enumerate(real_forward(values)):
                cos, sin = twid_ref[0, q : q + 1, :], twid_ref[1, q : q + 1, :]
                if im is None:
                    spec[q, r, :INNER] = re * cos
                    spec[q, r, INNER:] = -re * sin
                else:
                    spec[q, r, :INNER] = re * cos + im * sin
                    spec[q, r, INNER:] = im * cos - re * sin
            return k

        lax.fori_loop(0, tiles, analyse, 0)
        h = lax.rem(mine * upd + c, parts)
        full = dot3(spec[...].reshape(HALF * part_rows, 2 * INNER), fwd_ref)
        weight = damp_ref[h].reshape(HALF * part_rows, INNER)
        full = full * jnp.concatenate([weight, weight], axis=1)
        spec[...] = dot3(full, bwd_ref).reshape(HALF, part_rows, 2 * INNER)

        def synthesise(i, k):
            r = pl.ds(pl.multiple_of(i * 8, 8), 8)
            waves = []
            for q in range(HALF):
                cos, sin = twid_ref[0, q : q + 1, :], twid_ref[1, q : q + 1, :]
                re, im = spec[q, r, :INNER], spec[q, r, INNER:]
                waves.append((re * cos - im * sin, im * cos + re * sin))
            for p, value in enumerate(real_backward(waves)):
                done[c, p // per, r, (p % per) * INNER : (p % per + 1) * INNER] = value
            return k

        lax.fori_loop(0, tiles, synthesise, 0)
        lax.fori_loop(1, nj, lambda t, k: (back_copy(c, lax.rem(j + t, nj)).start(), k)[1], 0)

        @pl.when(active)
        def _():
            back_own(c).start()

        @pl.when(jnp.logical_not(active))
        def _():
            back_copy(c, j).start()

        return carry

    lax.fori_loop(0, upd, handle, 0)

    def settle(c, carry):
        lax.fori_loop(1, nj, lambda t, k: (back_copy(c, lax.rem(j + t, nj)).wait_send(), k)[1], 0)

        @pl.when(active)
        def _():
            def finish(t, k):
                out_copy(c, t).wait_send()
                back_wait(c, lax.rem(mine + t, count)).wait_recv()
                return k

            lax.fori_loop(1, count, finish, 0)
            back_own(c).wait()

        @pl.when(jnp.logical_not(active))
        def _():
            back_copy(c, j).wait_send()

        return carry

    lax.fori_loop(0, upd, settle, 0)


def constants():
    k = np.arange(HALF)[:, None]
    q = np.arange(INNER)[None, :]
    turn = 2 * np.pi * (k * q) / (OUTER * INNER)
    twiddle = np.stack([np.cos(turn), np.sin(turn)]).astype(np.float32)
    turn = 2 * np.pi * ((q.T * q) % INNER) / INNER
    cos, sin = np.cos(turn), np.sin(turn)
    forward = np.block([[cos, -sin], [sin, cos]])

    def pair(m):
        high = m.astype(jnp.bfloat16)
        return np.stack([high, (m - high.astype(np.float64)).astype(jnp.bfloat16)])

    return jnp.asarray(twiddle), jnp.asarray(pair(forward)), jnp.asarray(pair(forward.T))


def filter_circles(inc, weights, parts):
    nj = lax.axis_size("lon")
    stacks, rows, width = inc.shape
    upd = stacks * parts // (2 * nj)
    part_rows = rows // parts
    vmem = pl.BlockSpec(memory_space=pltpu.VMEM)
    hbm = pl.BlockSpec(memory_space=pl.ANY)
    dma = pltpu.SemaphoreType.DMA
    twiddle, forward, backward = constants()
    return pl.pallas_call(
        functools.partial(circle_kernel, upd, parts),
        out_shape=jax.ShapeDtypeStruct(inc.shape, jnp.float32),
        in_specs=[hbm, vmem, vmem, vmem, vmem],
        out_specs=hbm,
        scratch_shapes=[
            pltpu.VMEM((upd, nj, part_rows, width), jnp.float32),
            pltpu.VMEM((upd, nj, part_rows, width), jnp.float32),
            pltpu.VMEM((HALF, part_rows, 2 * INNER), jnp.float32),
            dma((upd, 2 * nj)),
            dma((upd, nj)),
            dma((upd, nj)),
            dma((upd, 2 * nj)),
        ],
        compiler_params=pltpu.CompilerParams(
            collective_id=1, has_side_effects=True, vmem_limit_bytes=40 * 1024 * 1024
        ),
        name="circles",
    )(inc, weights, twiddle, forward, backward)


def per_device(state, level_courant, damp_table, row_flag, row_table, partner):
    fields_n, levels_n, rows_n, cols_n = state.shape
    na = lax.axis_size("lat")
    a = lax.axis_index("lat")
    whole_rows = rows_n * na

    def geometry(row_pos):
        latitude = -jnp.pi / 2 + jnp.pi * (row_pos.astype(jnp.float32) + 0.5) / whole_rows
        return jnp.cos(latitude), jnp.sin(latitude)

    first_row = a * rows_n
    cos1, sin1 = geometry(first_row + jnp.arange(rows_n, dtype=jnp.int32))
    metric1 = 1.0 / jnp.maximum(cos1, cos_floor)
    geo = jnp.broadcast_to(jnp.stack([cos1, sin1, metric1])[:, :, None], (3, rows_n, INNER))
    cos_s, sin_s = geometry(first_row - 1)
    cos_n, sin_n = geometry(first_row + rows_n)
    south = a == 0
    ends = jnp.stack([
        cos_s, sin_s, cos_n, sin_n, jnp.where(south, cos1[0], cos1[-1]), jnp.where(south, sin1[0], sin1[-1])
    ])
    inc = increments_of(state, level_courant, partner, geo, ends)

    quarter = na // 4
    pairs = [(i, 2 * quarter - 1 - i if i < na // 2 else 2 * na - 2 * quarter - 1 - i) for i in range(na)]
    active = (a < quarter) | (a >= na - quarter)
    table = jnp.where(active, row_table, lax.ppermute(row_table, "lat", pairs))
    parts = 2
    count = damp_table.shape[0]
    length = OUTER * INNER
    full = jnp.concatenate(
        [jnp.ones((count, 1), jnp.float32), damp_table, jnp.flip(damp_table[:, :-1], axis=1)], axis=1
    )
    grid = jnp.transpose(full.reshape(count, INNER, OUTER), (0, 2, 1))[:, :HALF] * (1.0 / length)
    pick = (table[:, None] == jnp.arange(count, dtype=jnp.int32)[None, :]).astype(jnp.float32)
    weights = jnp.einsum(
        "hrt,tkm->hkrm", pick.reshape(parts, rows_n // parts, count), grid, precision=lax.Precision.HIGHEST
    )
    smooth = filter_circles(inc, weights, parts)
    chosen = (active & (row_flag == 1))[None, :, None]
    result = state.reshape(inc.shape) + jnp.where(chosen, smooth, inc)
    return result.reshape(state.shape)


def solution(mesh):
    placed = (P(None, None, "lat", "lon"), P(), P(), P("lat"), P("lat"), P("lon"))
    return jax.shard_map(
        per_device,
        mesh=mesh,
        in_specs=placed,
        out_specs=P(None, None, "lat", "lon"),
        check_vma=False,
    )
```

```python
import functools
import math

import jax
import jax.numpy as jnp
import numpy as np
from jax import lax
from jax.experimental import pallas as pl
from jax.experimental.pallas import tpu as pltpu
from jax.sharding import PartitionSpec as P

coriolis = 0.3
cos_floor = 0.25
MESH = pl.DeviceIdType.MESH
OUTER = 32
INNER = 128
HALF = OUTER // 2 + 1


def wide(tile, width):
    count = width // INNER
    return tile if count == 1 else jnp.concatenate([tile] * count, axis=1)


def step_kernel(
    c_ref, ends_ref, state_ref, geo_ref, ccol_ref, clane_ref, meet_ref, out_ref,
    inc_ref, out_sem, rows, cols, rows_in, cols_in, circle, eff, edge, side_cols, pad_p, pad_t, pad_f,
    lat_send, lat_recv, lon_send, lon_recv, cir_send, cir_recv,
):
    a, j = lax.axis_index("lat"), lax.axis_index("lon")
    na, nj = lax.axis_size("lat"), lax.axis_size("lon")
    levels, height, width = state_ref.shape[1:]
    barrier = pltpu.get_barrier_semaphore()

    def greet(t, carry):
        pl.semaphore_signal(barrier, inc=1, device_id=(a, lax.rem(j + t, nj)), device_id_type=MESH)
        return carry

    lax.fori_loop(1, nj, greet, 0)
    for near in (lax.rem(a + 1, na), lax.rem(a + na - 1, na)):
        pl.semaphore_signal(barrier, inc=1, device_id=(near, j), device_id_type=MESH)

    order = (0, 0, 1, 2, 3)
    for s in range(2):
        for k, f in enumerate(order):
            inner = 1 if k == 1 else 0
            r = inner if s == 0 else height - 1 - inner
            for l in range(levels):
                rows[s, 8 * k + l : 8 * k + l + 1, :] = state_ref[f, l, r : r + 1, :]
        rows[s, 40:48, :] = meet_ref[...]
    lane = lax.broadcasted_iota(jnp.int32, (height, INNER), 1)
    for s in range(2):
        packed = jnp.zeros((height, INNER), jnp.float32)
        for k, f in enumerate(order):
            inner = 1 if k == 1 else 0
            source = inner if s == 0 else INNER - 1 - inner
            start = 0 if s == 0 else width - INNER
            for l in range(levels):
                tile = state_ref[f, l, :, start : start + INNER]
                spot = 8 * k + l
                shift = (spot - source) % INNER
                if shift:
                    tile = pltpu.roll(tile, shift, 1)
                packed = jnp.where(lane == spot, tile, packed)
        cols[s] = packed
    pl.semaphore_wait(barrier, nj + 1)

    pole = jnp.logical_or(a == 0, a == na - 1)
    side = jnp.where(a == 0, 0, 1)

    def lat_copy(s):
        target = a - 1 if s == 0 else a + 1
        return pltpu.make_async_remote_copy(
            rows.at[s], rows_in.at[1 - s], lat_send.at[s], lat_recv.at[1 - s],
            device_id=(target, j), device_id_type=MESH)

    def lon_copy(s):
        target = lax.rem(j + (nj - 1 if s == 0 else 1), nj)
        return pltpu.make_async_remote_copy(
            cols.at[s], cols_in.at[1 - s], lon_send.at[s], lon_recv.at[1 - s],
            device_id=(a, target), device_id_type=MESH)

    def circle_copy(t):
        return pltpu.make_async_remote_copy(
            rows.at[side], circle.at[j], cir_send.at[t], cir_recv.at[j],
            device_id=(a, lax.rem(j + t, nj)), device_id_type=MESH)

    def circle_wait(t):
        source = lax.rem(j + t, nj)
        return pltpu.make_async_remote_copy(
            rows.at[side], circle.at[source], cir_send.at[t], cir_recv.at[source],
            device_id=(a, source), device_id_type=MESH)

    own = pltpu.make_async_copy(rows.at[side], circle.at[j], cir_recv.at[j])

    @pl.when(pole)
    def _():
        lax.fori_loop(1, nj, lambda t, c: (circle_copy(t).start(), c)[1], 0)
        own.start()

    @pl.when(a > 0)
    def _():
        lat_copy(0).start()

    @pl.when(a < na - 1)
    def _():
        lat_copy(1).start()

    lon_copy(0).start()
    lon_copy(1).start()

    @pl.when(a > 0)
    def _():
        lat_copy(0).wait_send()
        lat_copy(1).wait_recv()

    @pl.when(a < na - 1)
    def _():
        lat_copy(1).wait_send()
        lat_copy(0).wait_recv()

    ccol = wide(ccol_ref[...], width)

    for s in range(2):
        near, far, u, v, th = (rows_in[s, 8 * k : 8 * k + 8, :] for k in range(5))
        first = rows[s, 0:8, :]
        rise = first - far if s == 0 else far - first
        flux = (v + (-ccol * rise * 0.5 - coriolis * ends_ref[2 * s + 1] * u)) * ends_ref[2 * s]
        eff[s, 0:8, :] = near
        eff[s, 8:16, :] = th
        eff[s, 16:24, :] = flux

    @pl.when(pole)
    def _():
        def finish(t, carry):
            circle_copy(t).wait_send()
            circle_wait(t).wait_recv()
            return carry

        lax.fori_loop(1, nj, finish, 0)
        own.wait()
        column = lax.broadcasted_iota(jnp.int32, (width, width), 0)

        def gather(count, where):
            def add(s, total):
                x = circle[s, 0:count, :]
                high = x.astype(jnp.bfloat16).astype(jnp.float32)
                rest = x - high
                middle = rest.astype(jnp.bfloat16).astype(jnp.float32)
                pieces = jnp.concatenate([high, middle, rest - middle], axis=0).astype(jnp.bfloat16)
                hit = (column + s * width).astype(jnp.float32) == where
                chosen = jnp.where(hit, 1.0, 0.0).astype(jnp.bfloat16)
                return total + jnp.dot(pieces, chosen, preferred_element_type=jnp.float32)

            total = lax.fori_loop(0, nj, add, jnp.zeros((3 * count, width), jnp.float32))
            return (total[:count] + total[count : 2 * count]) + total[2 * count :]

        met = gather(48, meet_ref[0:1, :])
        twice = gather(8, met[40:41])
        near, inner, u, v, th = (met[8 * k : 8 * k + 8] for k in range(5))
        rise = jnp.where(a == 0, 1.0, -1.0) * (inner - twice)
        flux = -(v + (-ccol * rise * 0.5 - coriolis * ends_ref[5] * u)) * ends_ref[4]
        eff[side, 0:8, :] = near
        eff[side, 8:16, :] = th
        eff[side, 16:24, :] = flux

    lon_copy(0).wait()
    lon_copy(1).wait()

    for s in range(2):
        got = cols_in[s]
        first = cols[s]
        far, u, v = (pltpu.roll(got, INNER - 8 * k, 1) for k in (1, 2, 3))
        rise = first - far if s == 0 else far - first
        fresh = u + (-clane_ref[0:1, :] * geo_ref[2] * rise * 0.5 + coriolis * geo_ref[1] * v)
        edge[s] = jnp.where(lane < 40, got, pltpu.roll(fresh, 40, 1))

    lanes = lax.broadcasted_iota(jnp.int32, (8, width), 1)

    def leave(f, l):
        spot = f * levels + l
        return pltpu.make_async_copy(inc_ref.at[spot], out_ref.at[spot], out_sem.at[spot])

    def level(l, carry):
        c = c_ref[l]
        for k, lane0 in enumerate((0, 32, 40)):
            side_cols[2 * k] = pltpu.roll(edge[0], INNER - lane0 - l, 1)
            side_cols[2 * k + 1] = pltpu.roll(edge[1], INNER - 1 - lane0 - l, 1)
        inside = slice(8, 8 + height)
        pad_p[inside, :] = state_ref[0, l]
        pad_t[inside, :] = state_ref[3, l]
        for k, pad in enumerate((pad_p, pad_t, pad_f)):
            pad[7:8, :] = eff[0, pl.ds(8 * k + l, 1), :]
            pad[8 + height : 9 + height, :] = eff[1, pl.ds(8 * k + l, 1), :]

        def zonal(x, k, r):
            west = jnp.where(lanes == 0, wide(side_cols[2 * k, r, :], width), pltpu.roll(x, 1, 1))
            east = jnp.where(
                lanes == width - 1, wide(side_cols[2 * k + 1, r, :], width), pltpu.roll(x, width - 1, 1)
            )
            return east - west

        def merid(pad, i):
            return pad[9 + 8 * i : 17 + 8 * i, :] - pad[7 + 8 * i : 15 + 8 * i, :]

        for i in range(height // 8):
            r = slice(8 * i, 8 * i + 8)
            cos, sin, metric = (wide(geo_ref[k, r, :], width) for k in range(3))
            u, v = state_ref[1, l, r, :], state_ref[2, l, r, :]
            tend_u = -c * metric * zonal(state_ref[0, l, r, :], 0, r) * 0.5 + coriolis * sin * v
            tend_v = -c * merid(pad_p, i) * 0.5 - coriolis * sin * u
            u_new, v_new = u + tend_u, v + tend_v
            pad_f[8 + 8 * i : 16 + 8 * i, :] = v_new * cos
            inc_ref[levels + l, r, :] = tend_u
            inc_ref[2 * levels + l, r, :] = tend_v
            inc_ref[3 * levels + l, r, :] = (
                -c * metric * u_new * zonal(state_ref[3, l, r, :], 1, r) * 0.5 - c * v_new * merid(pad_t, i) * 0.5
            )
            inc_ref[l, r, :] = zonal(u_new, 2, r) * 0.5
        for i in range(height // 8):
            r = slice(8 * i, 8 * i + 8)
            metric = wide(geo_ref[2, r, :], width)
            inc_ref[l, r, :] = -(c * metric * (inc_ref[l, r, :] + merid(pad_f, i) * 0.5))
        for f in range(4):
            leave(f, l).start()
        return carry

    lax.fori_loop(0, levels, level, 0)

    def settle(l, carry):
        for f in range(4):
            leave(f, l).wait()
        return carry

    lax.fori_loop(0, levels, settle, 0)


def increments_of(state, level_courant, partner, geo, ends):
    fields, levels, height, width = state.shape
    nj = lax.axis_size("lon")
    vmem = pl.BlockSpec(memory_space=pltpu.VMEM)
    smem = pl.BlockSpec(memory_space=pltpu.SMEM)
    dma = pltpu.SemaphoreType.DMA
    f32 = jnp.float32
    ccol = jnp.broadcast_to(level_courant[:, None], (levels, INNER))
    clane = jnp.broadcast_to(jnp.pad(level_courant, (0, INNER - levels))[None], (8, INNER))
    meet = jnp.broadcast_to(partner.astype(f32)[None], (8, width))
    return pl.pallas_call(
        step_kernel,
        out_shape=jax.ShapeDtypeStruct((fields * levels, height, width), f32),
        in_specs=[smem, smem, vmem, vmem, vmem, vmem, vmem],
        out_specs=pl.BlockSpec(memory_space=pl.ANY),
        scratch_shapes=[
            pltpu.VMEM((fields * levels, height, width), f32),
            dma((fields * levels,)),
            pltpu.VMEM((2, 48, width), f32),
            pltpu.VMEM((2, height, INNER), f32),
            pltpu.VMEM((2, 48, width), f32),
            pltpu.VMEM((2, height, INNER), f32),
            pltpu.VMEM((nj, 48, width), f32),
            pltpu.VMEM((2, 24, width), f32),
            pltpu.VMEM((2, height, INNER), f32),
            pltpu.VMEM((6, height, INNER), f32),
            pltpu.VMEM((height + 16, width), f32),
            pltpu.VMEM((height + 16, width), f32),
            pltpu.VMEM((height + 16, width), f32),
            dma((2,)), dma((2,)), dma((2,)), dma((2,)), dma((nj,)), dma((nj,)),
        ],
        compiler_params=pltpu.CompilerParams(
            collective_id=0, has_side_effects=True, vmem_limit_bytes=58 * 1024 * 1024
        ),
        name="step",
    )(level_courant, ends, state, geo, ccol, clane, meet)


def real_forward(values):
    n = len(values)
    if n == 1:
        return [(values[0], None)]
    if n == 2:
        return [(values[0] + values[1], None), (values[0] - values[1], None)]
    even = real_forward(values[0::2])
    odd = real_forward(values[1::2])
    half = n // 2
    out = [None] * (half + 1)
    for k in range(half // 2 + 1):
        er, ei = even[k]
        orr, oi = odd[k]
        if k == 0:
            out[0] = (er + orr, None)
            out[half] = (er - orr, None)
            continue
        c, s = math.cos(2 * math.pi * k / n), math.sin(2 * math.pi * k / n)
        if k == half // 2:
            out[k] = (er, -orr)
            continue
        if oi is None:
            tr, ti = c * orr, -s * orr
        else:
            tr, ti = c * orr + s * oi, c * oi - s * orr
        eii = 0.0 if ei is None else ei
        out[k] = (er + tr, eii + ti)
        out[half - k] = (er - tr, ti - eii)
    return out


def real_backward(spec):
    n = 2 * (len(spec) - 1)
    if n == 2:
        return [spec[0][0] + spec[1][0], spec[0][0] - spec[1][0]]
    half = n // 2
    even, odd = [], []
    for k in range(half // 2 + 1):
        xr, xi = spec[k]
        yr, yi = spec[half - k]
        if k == 0:
            even.append((xr + yr, None))
            odd.append((xr - yr, None))
            continue
        if k == half // 2:
            even.append((2.0 * xr, None))
            odd.append((-2.0 * xi, None))
            continue
        c, s = math.cos(2 * math.pi * k / n), math.sin(2 * math.pi * k / n)
        dr, di = xr - yr, xi + yi
        even.append((xr + yr, xi - yi))
        odd.append((c * dr - s * di, c * di + s * dr))
    out = [None] * n
    out[0::2] = real_backward(even)
    out[1::2] = real_backward(odd)
    return out


def split(x):
    high = x.astype(jnp.bfloat16)
    return high, (x - high.astype(jnp.float32)).astype(jnp.bfloat16)


def dot3(x, w_ref):
    high, low = split(x)
    dot = functools.partial(jnp.dot, preferred_element_type=jnp.float32)
    return dot(high, w_ref[0]) + (dot(low, w_ref[0]) + dot(high, w_ref[1]))


def circle_kernel(upd, parts, inc_ref, damp_ref, twid_ref, fwd_ref, bwd_ref, out_ref, recv, done, spec, send1, recv1, send2, recv2):
    a, j = lax.axis_index("lat"), lax.axis_index("lon")
    na, nj = lax.axis_size("lat"), lax.axis_size("lon")
    quarter = na // 4
    low = a < na // 2
    active = jnp.logical_or(a < quarter, a >= na - quarter)
    mirror = jnp.where(low, 2 * quarter - 1 - a, 2 * na - 2 * quarter - 1 - a)
    source_lat = jnp.where(active, a, mirror)
    helper_lat = jnp.where(active, mirror, a)
    mine = jnp.where(active, j, nj + j)
    count = 2 * nj
    part_rows = recv.shape[2]
    width = recv.shape[3]

    def place(d):
        return (jnp.where(d < nj, source_lat, helper_lat), lax.rem(d, nj))

    def unit(ref, d, c):
        u = d * upd + c
        r = pl.multiple_of(lax.rem(u, parts) * part_rows, 8)
        return ref.at[u // parts, pl.ds(r, part_rows), :]

    barrier = pltpu.get_barrier_semaphore()

    def greet(t, carry):
        pl.semaphore_signal(barrier, inc=1, device_id=place(lax.rem(mine + t, count)), device_id_type=MESH)
        return carry

    lax.fori_loop(1, count, greet, 0)
    pl.semaphore_wait(barrier, count - 1)

    def out_copy(c, t):
        d = lax.rem(mine + t, count)
        return pltpu.make_async_remote_copy(
            unit(inc_ref, d, c), recv.at[c, j], send1.at[c, t], recv1.at[c, j],
            device_id=place(d), device_id_type=MESH)

    def out_own(c):
        return pltpu.make_async_copy(unit(inc_ref, mine, c), recv.at[c, j], recv1.at[c, j])

    def in_wait(c, s):
        return pltpu.make_async_remote_copy(
            unit(inc_ref, mine, c), recv.at[c, s], send1.at[c, 0], recv1.at[c, s],
            device_id=(source_lat, s), device_id_type=MESH)

    def back_copy(c, s):
        return pltpu.make_async_remote_copy(
            done.at[c, s], unit(out_ref, mine, c), send2.at[c, s], recv2.at[c, mine],
            device_id=(source_lat, s), device_id_type=MESH)

    def back_own(c):
        return pltpu.make_async_copy(done.at[c, j], unit(out_ref, mine, c), recv2.at[c, mine])

    def back_wait(c, d):
        return pltpu.make_async_remote_copy(
            done.at[c, j], unit(out_ref, d, c), send2.at[c, j], recv2.at[c, d],
            device_id=place(d), device_id_type=MESH)

    @pl.when(active)
    def _():
        def launch(c, carry):
            lax.fori_loop(1, count, lambda t, k: (out_copy(c, t).start(), k)[1], 0)
            out_own(c).start()
            return carry

        lax.fori_loop(0, upd, launch, 0)

    tiles = part_rows // 8
    per = width // INNER

    def handle(c, carry):
        def arrive(t, k):
            in_wait(c, lax.rem(j + t, nj)).wait_recv()
            return k

        lax.fori_loop(1, nj, arrive, 0)

        @pl.when(active)
        def _():
            out_own(c).wait()

        @pl.when(jnp.logical_not(active))
        def _():
            in_wait(c, j).wait_recv()

        def analyse(i, k):
            r = pl.ds(pl.multiple_of(i * 8, 8), 8)
            values = [
                recv[c, p // per, r, (p % per) * INNER : (p % per + 1) * INNER] for p in range(OUTER)
            ]
            for q, (re, im) in enumerate(real_forward(values)):
                cos, sin = twid_ref[0, q : q + 1, :], twid_ref[1, q : q + 1, :]
                if im is None:
                    spec[q, r, :INNER] = re * cos
                    spec[q, r, INNER:] = -re * sin
                else:
                    spec[q, r, :INNER] = re * cos + im * sin
                    spec[q, r, INNER:] = im * cos - re * sin
            return k

        lax.fori_loop(0, tiles, analyse, 0)
        h = lax.rem(mine * upd + c, parts)
        full = dot3(spec[...].reshape(HALF * part_rows, 2 * INNER), fwd_ref)
        weight = damp_ref[h].reshape(HALF * part_rows, INNER)
        full = full * jnp.concatenate([weight, weight], axis=1)
        spec[...] = dot3(full, bwd_ref).reshape(HALF, part_rows, 2 * INNER)

        def synthesise(i, k):
            r = pl.ds(pl.multiple_of(i * 8, 8), 8)
            waves = []
            for q in range(HALF):
                cos, sin = twid_ref[0, q : q + 1, :], twid_ref[1, q : q + 1, :]
                re, im = spec[q, r, :INNER], spec[q, r, INNER:]
                waves.append((re * cos - im * sin, im * cos + re * sin))
            for p, value in enumerate(real_backward(waves)):
                done[c, p // per, r, (p % per) * INNER : (p % per + 1) * INNER] = value
            return k

        lax.fori_loop(0, tiles, synthesise, 0)
        lax.fori_loop(1, nj, lambda t, k: (back_copy(c, lax.rem(j + t, nj)).start(), k)[1], 0)

        @pl.when(active)
        def _():
            back_own(c).start()

        @pl.when(jnp.logical_not(active))
        def _():
            back_copy(c, j).start()

        return carry

    lax.fori_loop(0, upd, handle, 0)

    def settle(c, carry):
        lax.fori_loop(1, nj, lambda t, k: (back_copy(c, lax.rem(j + t, nj)).wait_send(), k)[1], 0)

        @pl.when(active)
        def _():
            def finish(t, k):
                out_copy(c, t).wait_send()
                back_wait(c, lax.rem(mine + t, count)).wait_recv()
                return k

            lax.fori_loop(1, count, finish, 0)
            back_own(c).wait()

        @pl.when(jnp.logical_not(active))
        def _():
            back_copy(c, j).wait_send()

        return carry

    lax.fori_loop(0, upd, settle, 0)


def constants():
    k = np.arange(HALF)[:, None]
    q = np.arange(INNER)[None, :]
    turn = 2 * np.pi * (k * q) / (OUTER * INNER)
    twiddle = np.stack([np.cos(turn), np.sin(turn)]).astype(np.float32)
    turn = 2 * np.pi * ((q.T * q) % INNER) / INNER
    cos, sin = np.cos(turn), np.sin(turn)
    forward = np.block([[cos, -sin], [sin, cos]])

    def pair(m):
        high = m.astype(jnp.bfloat16)
        return np.stack([high, (m - high.astype(np.float64)).astype(jnp.bfloat16)])

    return jnp.asarray(twiddle), jnp.asarray(pair(forward)), jnp.asarray(pair(forward.T))


def filter_circles(inc, weights, parts):
    nj = lax.axis_size("lon")
    stacks, rows, width = inc.shape
    upd = stacks * parts // (2 * nj)
    part_rows = rows // parts
    vmem = pl.BlockSpec(memory_space=pltpu.VMEM)
    hbm = pl.BlockSpec(memory_space=pl.ANY)
    dma = pltpu.SemaphoreType.DMA
    twiddle, forward, backward = constants()
    return pl.pallas_call(
        functools.partial(circle_kernel, upd, parts),
        out_shape=jax.ShapeDtypeStruct(inc.shape, jnp.float32),
        in_specs=[hbm, vmem, vmem, vmem, vmem],
        out_specs=hbm,
        scratch_shapes=[
            pltpu.VMEM((upd, nj, part_rows, width), jnp.float32),
            pltpu.VMEM((upd, nj, part_rows, width), jnp.float32),
            pltpu.VMEM((HALF, part_rows, 2 * INNER), jnp.float32),
            dma((upd, 2 * nj)),
            dma((upd, nj)),
            dma((upd, nj)),
            dma((upd, 2 * nj)),
        ],
        compiler_params=pltpu.CompilerParams(
            collective_id=1, has_side_effects=True, vmem_limit_bytes=58 * 1024 * 1024
        ),
        name="circles",
    )(inc, weights, twiddle, forward, backward)


def per_device(state, level_courant, damp_table, row_flag, row_table, partner):
    fields_n, levels_n, rows_n, cols_n = state.shape
    na = lax.axis_size("lat")
    a = lax.axis_index("lat")
    whole_rows = rows_n * na

    def geometry(row_pos):
        latitude = -jnp.pi / 2 + jnp.pi * (row_pos.astype(jnp.float32) + 0.5) / whole_rows
        return jnp.cos(latitude), jnp.sin(latitude)

    first_row = a * rows_n
    cos1, sin1 = geometry(first_row + jnp.arange(rows_n, dtype=jnp.int32))
    metric1 = 1.0 / jnp.maximum(cos1, cos_floor)
    geo = jnp.broadcast_to(jnp.stack([cos1, sin1, metric1])[:, :, None], (3, rows_n, INNER))
    cos_s, sin_s = geometry(first_row - 1)
    cos_n, sin_n = geometry(first_row + rows_n)
    south = a == 0
    ends = jnp.stack([
        cos_s, sin_s, cos_n, sin_n, jnp.where(south, cos1[0], cos1[-1]), jnp.where(south, sin1[0], sin1[-1])
    ])
    inc = increments_of(state, level_courant, partner, geo, ends)

    quarter = na // 4
    pairs = [(i, 2 * quarter - 1 - i if i < na // 2 else 2 * na - 2 * quarter - 1 - i) for i in range(na)]
    active = (a < quarter) | (a >= na - quarter)
    table = jnp.where(active, row_table, lax.ppermute(row_table, "lat", pairs))
    parts = 2
    count = damp_table.shape[0]
    length = OUTER * INNER
    half = INNER // 2
    exact = lax.Precision.HIGHEST
    lower = jnp.concatenate([jnp.ones((count, 1), jnp.float32), damp_table[:, :-1]], axis=1)
    lower = jnp.transpose(lower.reshape(count, half, OUTER)[:, :, :HALF], (0, 2, 1))
    turned = damp_table.reshape(count, half, OUTER)[:, :, OUTER - HALF :]
    turn_m = jnp.asarray(np.eye(half, dtype=np.float32)[::-1].copy())
    turn_k = jnp.asarray(np.eye(HALF, dtype=np.float32)[::-1].copy())
    upper = jnp.einsum("tmj,jk,mn->tkn", turned, turn_k, turn_m, precision=exact)
    grid = jnp.concatenate([lower, upper], axis=2) * (1.0 / length)
    pick = (table[:, None] == jnp.arange(count, dtype=jnp.int32)[None, :]).astype(jnp.float32)
    weights = jnp.einsum(
        "hrt,tkm->hkrm", pick.reshape(parts, rows_n // parts, count), grid, precision=lax.Precision.HIGHEST
    )
    smooth = filter_circles(inc, weights, parts)
    chosen = (active & (row_flag == 1))[None, :, None]
    result = state.reshape(inc.shape) + jnp.where(chosen, smooth, inc)
    return result.reshape(state.shape)


def solution(mesh):
    placed = (P(None, None, "lat", "lon"), P(), P(), P("lat"), P("lat"), P("lon"))
    return jax.shard_map(
        per_device,
        mesh=mesh,
        in_specs=placed,
        out_specs=P(None, None, "lat", "lon"),
        check_vma=False,
    )
```

```python
import functools
import math

import jax
import jax.numpy as jnp
import numpy as np
from jax import lax
from jax.experimental import pallas as pl
from jax.experimental.pallas import tpu as pltpu
from jax.sharding import PartitionSpec as P

coriolis = 0.3
cos_floor = 0.25
MESH = pl.DeviceIdType.MESH
OUTER = 32
INNER = 128
HALF = OUTER // 2 + 1


def wide(tile, width):
    count = width // INNER
    return tile if count == 1 else jnp.concatenate([tile] * count, axis=1)


def step_kernel(
    c_ref, ends_ref, state_ref, geo_ref, ccol_ref, clane_ref, meet_ref, out_ref,
    inc_ref, out_sem, rows, cols, rows_in, cols_in, circle, eff, edge, side_cols, pad_p, pad_t, pad_f,
    lat_send, lat_recv, lon_send, lon_recv, cir_send, cir_recv,
):
    a, j = lax.axis_index("lat"), lax.axis_index("lon")
    na, nj = lax.axis_size("lat"), lax.axis_size("lon")
    levels, height, width = state_ref.shape[1:]
    barrier = pltpu.get_barrier_semaphore()

    def greet(t, carry):
        pl.semaphore_signal(barrier, inc=1, device_id=(a, lax.rem(j + t, nj)), device_id_type=MESH)
        return carry

    lax.fori_loop(1, nj, greet, 0)
    for near in (lax.rem(a + 1, na), lax.rem(a + na - 1, na)):
        pl.semaphore_signal(barrier, inc=1, device_id=(near, j), device_id_type=MESH)

    order = (0, 0, 1, 2, 3)
    for s in range(2):
        for k, f in enumerate(order):
            inner = 1 if k == 1 else 0
            r = inner if s == 0 else height - 1 - inner
            for l in range(levels):
                rows[s, 8 * k + l : 8 * k + l + 1, :] = state_ref[f, l, r : r + 1, :]
        rows[s, 40:48, :] = meet_ref[...]
    lane = lax.broadcasted_iota(jnp.int32, (height, INNER), 1)
    for s in range(2):
        packed = jnp.zeros((height, INNER), jnp.float32)
        for k, f in enumerate(order):
            inner = 1 if k == 1 else 0
            source = inner if s == 0 else INNER - 1 - inner
            start = 0 if s == 0 else width - INNER
            for l in range(levels):
                tile = state_ref[f, l, :, start : start + INNER]
                spot = 8 * k + l
                shift = (spot - source) % INNER
                if shift:
                    tile = pltpu.roll(tile, shift, 1)
                packed = jnp.where(lane == spot, tile, packed)
        cols[s] = packed
    pl.semaphore_wait(barrier, nj + 1)

    pole = jnp.logical_or(a == 0, a == na - 1)
    side = jnp.where(a == 0, 0, 1)

    def lat_copy(s):
        target = a - 1 if s == 0 else a + 1
        return pltpu.make_async_remote_copy(
            rows.at[s], rows_in.at[1 - s], lat_send.at[s], lat_recv.at[1 - s],
            device_id=(target, j), device_id_type=MESH)

    def lon_copy(s):
        target = lax.rem(j + (nj - 1 if s == 0 else 1), nj)
        return pltpu.make_async_remote_copy(
            cols.at[s], cols_in.at[1 - s], lon_send.at[s], lon_recv.at[1 - s],
            device_id=(a, target), device_id_type=MESH)

    def circle_copy(t):
        return pltpu.make_async_remote_copy(
            rows.at[side], circle.at[j], cir_send.at[t], cir_recv.at[j],
            device_id=(a, lax.rem(j + t, nj)), device_id_type=MESH)

    def circle_wait(t):
        source = lax.rem(j + t, nj)
        return pltpu.make_async_remote_copy(
            rows.at[side], circle.at[source], cir_send.at[t], cir_recv.at[source],
            device_id=(a, source), device_id_type=MESH)

    own = pltpu.make_async_copy(rows.at[side], circle.at[j], cir_recv.at[j])

    @pl.when(pole)
    def _():
        lax.fori_loop(1, nj, lambda t, c: (circle_copy(t).start(), c)[1], 0)
        own.start()

    @pl.when(a > 0)
    def _():
        lat_copy(0).start()

    @pl.when(a < na - 1)
    def _():
        lat_copy(1).start()

    lon_copy(0).start()
    lon_copy(1).start()

    @pl.when(a > 0)
    def _():
        lat_copy(0).wait_send()
        lat_copy(1).wait_recv()

    @pl.when(a < na - 1)
    def _():
        lat_copy(1).wait_send()
        lat_copy(0).wait_recv()

    ccol = wide(ccol_ref[...], width)

    for s in range(2):
        near, far, u, v, th = (rows_in[s, 8 * k : 8 * k + 8, :] for k in range(5))
        first = rows[s, 0:8, :]
        rise = first - far if s == 0 else far - first
        flux = (v + (-ccol * rise * 0.5 - coriolis * ends_ref[2 * s + 1] * u)) * ends_ref[2 * s]
        eff[s, 0:8, :] = near
        eff[s, 8:16, :] = th
        eff[s, 16:24, :] = flux

    @pl.when(pole)
    def _():
        def finish(t, carry):
            circle_copy(t).wait_send()
            circle_wait(t).wait_recv()
            return carry

        lax.fori_loop(1, nj, finish, 0)
        own.wait()
        column = lax.broadcasted_iota(jnp.int32, (width, width), 0)

        def gather(count, where):
            def add(s, total):
                x = circle[s, 0:count, :]
                high = x.astype(jnp.bfloat16).astype(jnp.float32)
                rest = x - high
                middle = rest.astype(jnp.bfloat16).astype(jnp.float32)
                pieces = jnp.concatenate([high, middle, rest - middle], axis=0).astype(jnp.bfloat16)
                hit = (column + s * width).astype(jnp.float32) == where
                chosen = jnp.where(hit, 1.0, 0.0).astype(jnp.bfloat16)
                return total + jnp.dot(pieces, chosen, preferred_element_type=jnp.float32)

            total = lax.fori_loop(0, nj, add, jnp.zeros((3 * count, width), jnp.float32))
            return (total[:count] + total[count : 2 * count]) + total[2 * count :]

        met = gather(48, meet_ref[0:1, :])
        twice = gather(8, met[40:41])
        near, inner, u, v, th = (met[8 * k : 8 * k + 8] for k in range(5))
        rise = jnp.where(a == 0, 1.0, -1.0) * (inner - twice)
        flux = -(v + (-ccol * rise * 0.5 - coriolis * ends_ref[5] * u)) * ends_ref[4]
        eff[side, 0:8, :] = near
        eff[side, 8:16, :] = th
        eff[side, 16:24, :] = flux

    lon_copy(0).wait()
    lon_copy(1).wait()

    for s in range(2):
        got = cols_in[s]
        first = cols[s]
        far, u, v = (pltpu.roll(got, INNER - 8 * k, 1) for k in (1, 2, 3))
        rise = first - far if s == 0 else far - first
        fresh = u + (-clane_ref[0:1, :] * geo_ref[2] * rise * 0.5 + coriolis * geo_ref[1] * v)
        edge[s] = jnp.where(lane < 40, got, pltpu.roll(fresh, 40, 1))

    lanes = lax.broadcasted_iota(jnp.int32, (8, width), 1)

    def leave(f, l):
        spot = f * levels + l
        return pltpu.make_async_copy(inc_ref.at[spot], out_ref.at[spot], out_sem.at[spot])

    def level(l, carry):
        c = c_ref[l]
        for k, lane0 in enumerate((0, 32, 40)):
            side_cols[2 * k] = pltpu.roll(edge[0], INNER - lane0 - l, 1)
            side_cols[2 * k + 1] = pltpu.roll(edge[1], INNER - 1 - lane0 - l, 1)
        inside = slice(8, 8 + height)
        pad_p[inside, :] = state_ref[0, l]
        pad_t[inside, :] = state_ref[3, l]
        for k, pad in enumerate((pad_p, pad_t, pad_f)):
            pad[7:8, :] = eff[0, pl.ds(8 * k + l, 1), :]
            pad[8 + height : 9 + height, :] = eff[1, pl.ds(8 * k + l, 1), :]

        def zonal(x, k, r):
            west = jnp.where(lanes == 0, wide(side_cols[2 * k, r, :], width), pltpu.roll(x, 1, 1))
            east = jnp.where(
                lanes == width - 1, wide(side_cols[2 * k + 1, r, :], width), pltpu.roll(x, width - 1, 1)
            )
            return east - west

        def merid(pad, i):
            return pad[9 + 8 * i : 17 + 8 * i, :] - pad[7 + 8 * i : 15 + 8 * i, :]

        for i in range(height // 8):
            r = slice(8 * i, 8 * i + 8)
            cos, sin, metric = (wide(geo_ref[k, r, :], width) for k in range(3))
            u, v = state_ref[1, l, r, :], state_ref[2, l, r, :]
            tend_u = -c * metric * zonal(state_ref[0, l, r, :], 0, r) * 0.5 + coriolis * sin * v
            tend_v = -c * merid(pad_p, i) * 0.5 - coriolis * sin * u
            u_new, v_new = u + tend_u, v + tend_v
            pad_f[8 + 8 * i : 16 + 8 * i, :] = v_new * cos
            inc_ref[levels + l, r, :] = tend_u
            inc_ref[2 * levels + l, r, :] = tend_v
            inc_ref[3 * levels + l, r, :] = (
                -c * metric * u_new * zonal(state_ref[3, l, r, :], 1, r) * 0.5 - c * v_new * merid(pad_t, i) * 0.5
            )
            inc_ref[l, r, :] = zonal(u_new, 2, r) * 0.5
        for i in range(height // 8):
            r = slice(8 * i, 8 * i + 8)
            metric = wide(geo_ref[2, r, :], width)
            inc_ref[l, r, :] = -(c * metric * (inc_ref[l, r, :] + merid(pad_f, i) * 0.5))
        for f in range(4):
            leave(f, l).start()
        return carry

    lax.fori_loop(0, levels, level, 0)

    def settle(l, carry):
        for f in range(4):
            leave(f, l).wait()
        return carry

    lax.fori_loop(0, levels, settle, 0)


def increments_of(state, level_courant, partner, geo, ends):
    fields, levels, height, width = state.shape
    nj = lax.axis_size("lon")
    vmem = pl.BlockSpec(memory_space=pltpu.VMEM)
    smem = pl.BlockSpec(memory_space=pltpu.SMEM)
    dma = pltpu.SemaphoreType.DMA
    f32 = jnp.float32
    ccol = jnp.broadcast_to(level_courant[:, None], (levels, INNER))
    clane = jnp.broadcast_to(jnp.pad(level_courant, (0, INNER - levels))[None], (8, INNER))
    meet = jnp.broadcast_to(partner.astype(f32)[None], (8, width))
    return pl.pallas_call(
        step_kernel,
        out_shape=jax.ShapeDtypeStruct((fields * levels, height, width), f32),
        in_specs=[smem, smem, vmem, vmem, vmem, vmem, vmem],
        out_specs=pl.BlockSpec(memory_space=pl.ANY),
        scratch_shapes=[
            pltpu.VMEM((fields * levels, height, width), f32),
            dma((fields * levels,)),
            pltpu.VMEM((2, 48, width), f32),
            pltpu.VMEM((2, height, INNER), f32),
            pltpu.VMEM((2, 48, width), f32),
            pltpu.VMEM((2, height, INNER), f32),
            pltpu.VMEM((nj, 48, width), f32),
            pltpu.VMEM((2, 24, width), f32),
            pltpu.VMEM((2, height, INNER), f32),
            pltpu.VMEM((6, height, INNER), f32),
            pltpu.VMEM((height + 16, width), f32),
            pltpu.VMEM((height + 16, width), f32),
            pltpu.VMEM((height + 16, width), f32),
            dma((2,)), dma((2,)), dma((2,)), dma((2,)), dma((nj,)), dma((nj,)),
        ],
        compiler_params=pltpu.CompilerParams(
            collective_id=0, has_side_effects=True, vmem_limit_bytes=58 * 1024 * 1024
        ),
        name="step",
    )(level_courant, ends, state, geo, ccol, clane, meet)


def real_forward(values):
    n = len(values)
    if n == 1:
        return [(values[0], None)]
    if n == 2:
        return [(values[0] + values[1], None), (values[0] - values[1], None)]
    even = real_forward(values[0::2])
    odd = real_forward(values[1::2])
    half = n // 2
    out = [None] * (half + 1)
    for k in range(half // 2 + 1):
        er, ei = even[k]
        orr, oi = odd[k]
        if k == 0:
            out[0] = (er + orr, None)
            out[half] = (er - orr, None)
            continue
        c, s = math.cos(2 * math.pi * k / n), math.sin(2 * math.pi * k / n)
        if k == half // 2:
            out[k] = (er, -orr)
            continue
        if oi is None:
            tr, ti = c * orr, -s * orr
        else:
            tr, ti = c * orr + s * oi, c * oi - s * orr
        eii = 0.0 if ei is None else ei
        out[k] = (er + tr, eii + ti)
        out[half - k] = (er - tr, ti - eii)
    return out


def real_backward(spec):
    n = 2 * (len(spec) - 1)
    if n == 2:
        return [spec[0][0] + spec[1][0], spec[0][0] - spec[1][0]]
    half = n // 2
    even, odd = [], []
    for k in range(half // 2 + 1):
        xr, xi = spec[k]
        yr, yi = spec[half - k]
        if k == 0:
            even.append((xr + yr, None))
            odd.append((xr - yr, None))
            continue
        if k == half // 2:
            even.append((2.0 * xr, None))
            odd.append((-2.0 * xi, None))
            continue
        c, s = math.cos(2 * math.pi * k / n), math.sin(2 * math.pi * k / n)
        dr, di = xr - yr, xi + yi
        even.append((xr + yr, xi - yi))
        odd.append((c * dr - s * di, c * di + s * dr))
    out = [None] * n
    out[0::2] = real_backward(even)
    out[1::2] = real_backward(odd)
    return out


def split(x):
    high = x.astype(jnp.bfloat16)
    return high, (x - high.astype(jnp.float32)).astype(jnp.bfloat16)


def dot3(x, w_ref):
    high, low = split(x)
    dot = functools.partial(jnp.dot, preferred_element_type=jnp.float32)
    return dot(high, w_ref[0]) + (dot(low, w_ref[0]) + dot(high, w_ref[1]))


def circle_kernel(upd, parts, inc_ref, damp_ref, twid_ref, fwd_ref, bwd_ref, out_ref, recv, done, spec, send1, recv1, send2, recv2):
    a, j = lax.axis_index("lat"), lax.axis_index("lon")
    na, nj = lax.axis_size("lat"), lax.axis_size("lon")
    quarter = na // 4
    low = a < na // 2
    active = jnp.logical_or(a < quarter, a >= na - quarter)
    mirror = jnp.where(low, 2 * quarter - 1 - a, 2 * na - 2 * quarter - 1 - a)
    source_lat = jnp.where(active, a, mirror)
    helper_lat = jnp.where(active, mirror, a)
    mine = jnp.where(active, j, nj + j)
    count = 2 * nj
    part_rows = recv.shape[2]
    width = recv.shape[3]

    def place(d):
        return (jnp.where(d < nj, source_lat, helper_lat), lax.rem(d, nj))

    def unit(ref, d, c):
        u = d * upd + c
        r = pl.multiple_of(lax.rem(u, parts) * part_rows, 8)
        return ref.at[u // parts, pl.ds(r, part_rows), :]

    barrier = pltpu.get_barrier_semaphore()

    def greet(t, carry):
        pl.semaphore_signal(barrier, inc=1, device_id=place(lax.rem(mine + t, count)), device_id_type=MESH)
        return carry

    lax.fori_loop(1, count, greet, 0)
    pl.semaphore_wait(barrier, count - 1)

    def out_copy(c, t):
        d = lax.rem(mine + t, count)
        return pltpu.make_async_remote_copy(
            unit(inc_ref, d, c), recv.at[c, j], send1.at[c, t], recv1.at[c, j],
            device_id=place(d), device_id_type=MESH)

    def out_own(c):
        return pltpu.make_async_copy(unit(inc_ref, mine, c), recv.at[c, j], recv1.at[c, j])

    def in_wait(c, s):
        return pltpu.make_async_remote_copy(
            unit(inc_ref, mine, c), recv.at[c, s], send1.at[c, 0], recv1.at[c, s],
            device_id=(source_lat, s), device_id_type=MESH)

    def back_copy(c, s):
        return pltpu.make_async_remote_copy(
            done.at[c, s], unit(out_ref, mine, c), send2.at[c, s], recv2.at[c, mine],
            device_id=(source_lat, s), device_id_type=MESH)

    def back_own(c):
        return pltpu.make_async_copy(done.at[c, j], unit(out_ref, mine, c), recv2.at[c, mine])

    def back_wait(c, d):
        return pltpu.make_async_remote_copy(
            done.at[c, j], unit(out_ref, d, c), send2.at[c, j], recv2.at[c, d],
            device_id=place(d), device_id_type=MESH)

    @pl.when(active)
    def _():
        def launch(c, carry):
            lax.fori_loop(1, count, lambda t, k: (out_copy(c, t).start(), k)[1], 0)
            out_own(c).start()
            return carry

        lax.fori_loop(0, upd, launch, 0)

    tiles = part_rows // 8
    per = width // INNER

    def handle(c, carry):
        def arrive(t, k):
            in_wait(c, lax.rem(j + t, nj)).wait_recv()
            return k

        lax.fori_loop(1, nj, arrive, 0)

        @pl.when(active)
        def _():
            out_own(c).wait()

        @pl.when(jnp.logical_not(active))
        def _():
            in_wait(c, j).wait_recv()

        def analyse(i, k):
            r = pl.ds(pl.multiple_of(i * 8, 8), 8)
            values = [
                recv[c, p // per, r, (p % per) * INNER : (p % per + 1) * INNER] for p in range(OUTER)
            ]
            for q, (re, im) in enumerate(real_forward(values)):
                cos, sin = twid_ref[0, q : q + 1, :], twid_ref[1, q : q + 1, :]
                if im is None:
                    spec[q, r, :INNER] = re * cos
                    spec[q, r, INNER:] = -re * sin
                else:
                    spec[q, r, :INNER] = re * cos + im * sin
                    spec[q, r, INNER:] = im * cos - re * sin
            return k

        lax.fori_loop(0, tiles, analyse, 0)
        h = lax.rem(mine * upd + c, parts)
        full = dot3(spec[...].reshape(HALF * part_rows, 2 * INNER), fwd_ref)
        weight = damp_ref[h].reshape(HALF * part_rows, INNER)
        full = full * jnp.concatenate([weight, weight], axis=1)
        spec[...] = dot3(full, bwd_ref).reshape(HALF, part_rows, 2 * INNER)

        def synthesise(i, k):
            r = pl.ds(pl.multiple_of(i * 8, 8), 8)
            waves = []
            for q in range(HALF):
                cos, sin = twid_ref[0, q : q + 1, :], twid_ref[1, q : q + 1, :]
                re, im = spec[q, r, :INNER], spec[q, r, INNER:]
                waves.append((re * cos - im * sin, im * cos + re * sin))
            for p, value in enumerate(real_backward(waves)):
                done[c, p // per, r, (p % per) * INNER : (p % per + 1) * INNER] = value
            return k

        lax.fori_loop(0, tiles, synthesise, 0)
        lax.fori_loop(1, nj, lambda t, k: (back_copy(c, lax.rem(j + t, nj)).start(), k)[1], 0)

        @pl.when(active)
        def _():
            back_own(c).start()

        @pl.when(jnp.logical_not(active))
        def _():
            back_copy(c, j).start()

        return carry

    lax.fori_loop(0, upd, handle, 0)

    def settle(c, carry):
        lax.fori_loop(1, nj, lambda t, k: (back_copy(c, lax.rem(j + t, nj)).wait_send(), k)[1], 0)

        @pl.when(active)
        def _():
            def finish(t, k):
                out_copy(c, t).wait_send()
                back_wait(c, lax.rem(mine + t, count)).wait_recv()
                return k

            lax.fori_loop(1, count, finish, 0)
            back_own(c).wait()

        @pl.when(jnp.logical_not(active))
        def _():
            back_copy(c, j).wait_send()

        return carry

    lax.fori_loop(0, upd, settle, 0)


def constants():
    k = np.arange(HALF)[:, None]
    q = np.arange(INNER)[None, :]
    turn = 2 * np.pi * (k * q) / (OUTER * INNER)
    twiddle = np.stack([np.cos(turn), np.sin(turn)]).astype(np.float32)
    turn = 2 * np.pi * ((q.T * q) % INNER) / INNER
    cos, sin = np.cos(turn), np.sin(turn)
    forward = np.block([[cos, -sin], [sin, cos]])

    def pair(m):
        high = m.astype(jnp.bfloat16)
        return np.stack([high, (m - high.astype(np.float64)).astype(jnp.bfloat16)])

    return jnp.asarray(twiddle), jnp.asarray(pair(forward)), jnp.asarray(pair(forward.T))


def filter_circles(inc, weights, parts, ident):
    nj = lax.axis_size("lon")
    stacks, rows, width = inc.shape
    upd = stacks * parts // (2 * nj)
    part_rows = rows // parts
    vmem = pl.BlockSpec(memory_space=pltpu.VMEM)
    hbm = pl.BlockSpec(memory_space=pl.ANY)
    dma = pltpu.SemaphoreType.DMA
    twiddle, forward, backward = constants()
    return pl.pallas_call(
        functools.partial(circle_kernel, upd, parts),
        out_shape=jax.ShapeDtypeStruct(inc.shape, jnp.float32),
        in_specs=[hbm, vmem, vmem, vmem, vmem],
        out_specs=hbm,
        scratch_shapes=[
            pltpu.VMEM((upd, nj, part_rows, width), jnp.float32),
            pltpu.VMEM((upd, nj, part_rows, width), jnp.float32),
            pltpu.VMEM((HALF, part_rows, 2 * INNER), jnp.float32),
            dma((upd, 2 * nj)),
            dma((upd, nj)),
            dma((upd, nj)),
            dma((upd, 2 * nj)),
        ],
        compiler_params=pltpu.CompilerParams(
            collective_id=ident, has_side_effects=True, vmem_limit_bytes=58 * 1024 * 1024
        ),
        name=f"circles{rows}",
    )(inc, weights, twiddle, forward, backward)


def per_device(state, level_courant, damp_table, row_flag, row_table, partner):
    fields_n, levels_n, rows_n, cols_n = state.shape
    na = lax.axis_size("lat")
    a = lax.axis_index("lat")
    whole_rows = rows_n * na

    def geometry(row_pos):
        latitude = -jnp.pi / 2 + jnp.pi * (row_pos.astype(jnp.float32) + 0.5) / whole_rows
        return jnp.cos(latitude), jnp.sin(latitude)

    first_row = a * rows_n
    cos1, sin1 = geometry(first_row + jnp.arange(rows_n, dtype=jnp.int32))
    metric1 = 1.0 / jnp.maximum(cos1, cos_floor)
    geo = jnp.broadcast_to(jnp.stack([cos1, sin1, metric1])[:, :, None], (3, rows_n, INNER))
    cos_s, sin_s = geometry(first_row - 1)
    cos_n, sin_n = geometry(first_row + rows_n)
    south = a == 0
    ends = jnp.stack([
        cos_s, sin_s, cos_n, sin_n, jnp.where(south, cos1[0], cos1[-1]), jnp.where(south, sin1[0], sin1[-1])
    ])
    inc = increments_of(state, level_courant, partner, geo, ends)

    quarter = na // 4
    pairs = [(i, 2 * quarter - 1 - i if i < na // 2 else 2 * na - 2 * quarter - 1 - i) for i in range(na)]
    active = (a < quarter) | (a >= na - quarter)
    codes = jnp.stack([row_flag, row_table])
    codes = jnp.where(active, codes, lax.ppermute(codes, "lat", pairs))
    flagged, table = codes[0] == 1, codes[1]
    bands = lax.all_gather(row_flag, "lat")
    fullest = jnp.max(jnp.sum((bands == 1).astype(jnp.int32), axis=1))
    count = damp_table.shape[0]
    length = OUTER * INNER
    half = INNER // 2
    exact = lax.Precision.HIGHEST
    lower = jnp.concatenate([jnp.ones((count, 1), jnp.float32), damp_table[:, :-1]], axis=1)
    lower = jnp.transpose(lower.reshape(count, half, OUTER)[:, :, :HALF], (0, 2, 1))
    turned = damp_table.reshape(count, half, OUTER)[:, :, OUTER - HALF :]
    turn_m = jnp.asarray(np.eye(half, dtype=np.float32)[::-1].copy())
    turn_k = jnp.asarray(np.eye(HALF, dtype=np.float32)[::-1].copy())
    upper = jnp.einsum("tmj,jk,mn->tkn", turned, turn_k, turn_m, precision=exact)
    grid = jnp.concatenate([lower, upper], axis=2) * (1.0 / length)
    pick = (table[:, None] == jnp.arange(count, dtype=jnp.int32)[None, :]).astype(jnp.float32)
    rank = jnp.cumsum(flagged.astype(jnp.int32)) - 1
    spots = jnp.arange(rows_n, dtype=jnp.int32)
    packing = ((rank[None, :] == spots[:, None]) & flagged[None, :]).astype(jnp.float32)
    fewest = max(1, lax.axis_size("lon") * 2 // (fields_n * levels_n))
    unit = 8 * fewest
    sizes = [rows_n * 11 // 14 // unit * unit, rows_n * 12 // 14 // unit * unit, rows_n]

    def smoothed(ident, kept, inc):
        parts = fewest if kept % 16 else 2
        mover = None if kept == rows_n else packing[:kept]
        choice = pick if mover is None else jnp.dot(mover, pick, precision=exact)
        weights = jnp.einsum(
            "hrt,tkm->hkrm", choice.reshape(parts, kept // parts, count), grid, precision=exact
        )
        if mover is None:
            return filter_circles(inc, weights, parts, ident)
        packed = jnp.einsum("kr,frw->fkw", mover, inc, precision=exact)
        packed = filter_circles(packed, weights, parts, ident)
        return jnp.einsum("kr,fkw->frw", mover, packed, precision=exact)

    branch = sum((fullest > size).astype(jnp.int32) for size in sizes[:-1])
    smooth = lax.switch(
        branch, [functools.partial(smoothed, 1 + n, size) for n, size in enumerate(sizes)], inc
    )
    chosen = (active & (row_flag == 1))[None, :, None]
    result = state.reshape(inc.shape) + jnp.where(chosen, smooth, inc)
    return result.reshape(state.shape)


def solution(mesh):
    placed = (P(None, None, "lat", "lon"), P(), P(), P("lat"), P("lat"), P("lon"))
    return jax.shard_map(
        per_device,
        mesh=mesh,
        in_specs=placed,
        out_specs=P(None, None, "lat", "lon"),
        check_vma=False,
    )
```

```python
import functools
import math

import jax
import jax.numpy as jnp
import numpy as np
from jax import lax
from jax.experimental import pallas as pl
from jax.experimental.pallas import tpu as pltpu
from jax.sharding import PartitionSpec as P

coriolis = 0.3
cos_floor = 0.25
MESH = pl.DeviceIdType.MESH
OUTER = 32
INNER = 128
HALF = OUTER // 2 + 1


def wide(tile, width):
    count = width // INNER
    return tile if count == 1 else jnp.concatenate([tile] * count, axis=1)


def step_kernel(
    c_ref, ends_ref, state_ref, geo_ref, ccol_ref, clane_ref, meet_ref, out_ref,
    inc_ref, out_sem, rows, cols, rows_in, cols_in, circle, eff, edge, side_cols, pad_p, pad_t, pad_f,
    lat_send, lat_recv, lon_send, lon_recv, cir_send, cir_recv,
):
    a, j = lax.axis_index("lat"), lax.axis_index("lon")
    na, nj = lax.axis_size("lat"), lax.axis_size("lon")
    levels, height, width = state_ref.shape[1:]
    barrier = pltpu.get_barrier_semaphore()

    def greet(t, carry):
        pl.semaphore_signal(barrier, inc=1, device_id=(a, lax.rem(j + t, nj)), device_id_type=MESH)
        return carry

    lax.fori_loop(1, nj, greet, 0)
    for near in (lax.rem(a + 1, na), lax.rem(a + na - 1, na)):
        pl.semaphore_signal(barrier, inc=1, device_id=(near, j), device_id_type=MESH)

    order = (0, 0, 1, 2, 3)
    for s in range(2):
        for k, f in enumerate(order):
            inner = 1 if k == 1 else 0
            r = inner if s == 0 else height - 1 - inner
            for l in range(levels):
                rows[s, 8 * k + l : 8 * k + l + 1, :] = state_ref[f, l, r : r + 1, :]
        rows[s, 40:48, :] = meet_ref[...]
    lane = lax.broadcasted_iota(jnp.int32, (height, INNER), 1)
    for s in range(2):
        packed = jnp.zeros((height, INNER), jnp.float32)
        for k, f in enumerate(order):
            inner = 1 if k == 1 else 0
            source = inner if s == 0 else INNER - 1 - inner
            start = 0 if s == 0 else width - INNER
            for l in range(levels):
                tile = state_ref[f, l, :, start : start + INNER]
                spot = 8 * k + l
                shift = (spot - source) % INNER
                if shift:
                    tile = pltpu.roll(tile, shift, 1)
                packed = jnp.where(lane == spot, tile, packed)
        cols[s] = packed
    pl.semaphore_wait(barrier, nj + 1)

    pole = jnp.logical_or(a == 0, a == na - 1)
    side = jnp.where(a == 0, 0, 1)

    def lat_copy(s):
        target = a - 1 if s == 0 else a + 1
        return pltpu.make_async_remote_copy(
            rows.at[s], rows_in.at[1 - s], lat_send.at[s], lat_recv.at[1 - s],
            device_id=(target, j), device_id_type=MESH)

    def lon_copy(s):
        target = lax.rem(j + (nj - 1 if s == 0 else 1), nj)
        return pltpu.make_async_remote_copy(
            cols.at[s], cols_in.at[1 - s], lon_send.at[s], lon_recv.at[1 - s],
            device_id=(a, target), device_id_type=MESH)

    def circle_copy(t):
        return pltpu.make_async_remote_copy(
            rows.at[side], circle.at[j], cir_send.at[t], cir_recv.at[j],
            device_id=(a, lax.rem(j + t, nj)), device_id_type=MESH)

    def circle_wait(t):
        source = lax.rem(j + t, nj)
        return pltpu.make_async_remote_copy(
            rows.at[side], circle.at[source], cir_send.at[t], cir_recv.at[source],
            device_id=(a, source), device_id_type=MESH)

    own = pltpu.make_async_copy(rows.at[side], circle.at[j], cir_recv.at[j])

    @pl.when(pole)
    def _():
        lax.fori_loop(1, nj, lambda t, c: (circle_copy(t).start(), c)[1], 0)
        own.start()

    @pl.when(a > 0)
    def _():
        lat_copy(0).start()

    @pl.when(a < na - 1)
    def _():
        lat_copy(1).start()

    lon_copy(0).start()
    lon_copy(1).start()

    @pl.when(a > 0)
    def _():
        lat_copy(0).wait_send()
        lat_copy(1).wait_recv()

    @pl.when(a < na - 1)
    def _():
        lat_copy(1).wait_send()
        lat_copy(0).wait_recv()

    ccol = wide(ccol_ref[...], width)

    for s in range(2):
        near, far, u, v, th = (rows_in[s, 8 * k : 8 * k + 8, :] for k in range(5))
        first = rows[s, 0:8, :]
        rise = first - far if s == 0 else far - first
        flux = (v + (-ccol * rise * 0.5 - coriolis * ends_ref[2 * s + 1] * u)) * ends_ref[2 * s]
        eff[s, 0:8, :] = near
        eff[s, 8:16, :] = th
        eff[s, 16:24, :] = flux

    @pl.when(pole)
    def _():
        def finish(t, carry):
            circle_copy(t).wait_send()
            circle_wait(t).wait_recv()
            return carry

        lax.fori_loop(1, nj, finish, 0)
        own.wait()
        column = lax.broadcasted_iota(jnp.int32, (width, width), 0)

        def gather(count, where):
            def add(s, total):
                x = circle[s, 0:count, :]
                high = x.astype(jnp.bfloat16).astype(jnp.float32)
                rest = x - high
                middle = rest.astype(jnp.bfloat16).astype(jnp.float32)
                pieces = jnp.concatenate([high, middle, rest - middle], axis=0).astype(jnp.bfloat16)
                hit = (column + s * width).astype(jnp.float32) == where
                chosen = jnp.where(hit, 1.0, 0.0).astype(jnp.bfloat16)
                return total + jnp.dot(pieces, chosen, preferred_element_type=jnp.float32)

            total = lax.fori_loop(0, nj, add, jnp.zeros((3 * count, width), jnp.float32))
            return (total[:count] + total[count : 2 * count]) + total[2 * count :]

        met = gather(48, meet_ref[0:1, :])
        twice = gather(8, met[40:41])
        near, inner, u, v, th = (met[8 * k : 8 * k + 8] for k in range(5))
        rise = jnp.where(a == 0, 1.0, -1.0) * (inner - twice)
        flux = -(v + (-ccol * rise * 0.5 - coriolis * ends_ref[5] * u)) * ends_ref[4]
        eff[side, 0:8, :] = near
        eff[side, 8:16, :] = th
        eff[side, 16:24, :] = flux

    lon_copy(0).wait()
    lon_copy(1).wait()

    for s in range(2):
        got = cols_in[s]
        first = cols[s]
        far, u, v = (pltpu.roll(got, INNER - 8 * k, 1) for k in (1, 2, 3))
        rise = first - far if s == 0 else far - first
        fresh = u + (-clane_ref[0:1, :] * geo_ref[2] * rise * 0.5 + coriolis * geo_ref[1] * v)
        edge[s] = jnp.where(lane < 40, got, pltpu.roll(fresh, 40, 1))

    lanes = lax.broadcasted_iota(jnp.int32, (8, width), 1)

    def leave(f, l):
        spot = f * levels + l
        return pltpu.make_async_copy(inc_ref.at[spot], out_ref.at[spot], out_sem.at[spot])

    def level(l, carry):
        c = c_ref[l]
        for k, lane0 in enumerate((0, 32, 40)):
            side_cols[2 * k] = pltpu.roll(edge[0], INNER - lane0 - l, 1)
            side_cols[2 * k + 1] = pltpu.roll(edge[1], INNER - 1 - lane0 - l, 1)
        inside = slice(8, 8 + height)
        pad_p[inside, :] = state_ref[0, l]
        pad_t[inside, :] = state_ref[3, l]
        for k, pad in enumerate((pad_p, pad_t, pad_f)):
            pad[7:8, :] = eff[0, pl.ds(8 * k + l, 1), :]
            pad[8 + height : 9 + height, :] = eff[1, pl.ds(8 * k + l, 1), :]

        def zonal(x, k, r):
            west = jnp.where(lanes == 0, wide(side_cols[2 * k, r, :], width), pltpu.roll(x, 1, 1))
            east = jnp.where(
                lanes == width - 1, wide(side_cols[2 * k + 1, r, :], width), pltpu.roll(x, width - 1, 1)
            )
            return east - west

        def merid(pad, i):
            return pad[9 + 8 * i : 17 + 8 * i, :] - pad[7 + 8 * i : 15 + 8 * i, :]

        for i in range(height // 8):
            r = slice(8 * i, 8 * i + 8)
            cos, sin, metric = (wide(geo_ref[k, r, :], width) for k in range(3))
            u, v = state_ref[1, l, r, :], state_ref[2, l, r, :]
            tend_u = -c * metric * zonal(state_ref[0, l, r, :], 0, r) * 0.5 + coriolis * sin * v
            tend_v = -c * merid(pad_p, i) * 0.5 - coriolis * sin * u
            u_new, v_new = u + tend_u, v + tend_v
            pad_f[8 + 8 * i : 16 + 8 * i, :] = v_new * cos
            inc_ref[levels + l, r, :] = tend_u
            inc_ref[2 * levels + l, r, :] = tend_v
            inc_ref[3 * levels + l, r, :] = (
                -c * metric * u_new * zonal(state_ref[3, l, r, :], 1, r) * 0.5 - c * v_new * merid(pad_t, i) * 0.5
            )
            inc_ref[l, r, :] = zonal(u_new, 2, r) * 0.5
        for i in range(height // 8):
            r = slice(8 * i, 8 * i + 8)
            metric = wide(geo_ref[2, r, :], width)
            inc_ref[l, r, :] = -(c * metric * (inc_ref[l, r, :] + merid(pad_f, i) * 0.5))
        for f in range(4):
            leave(f, l).start()
        return carry

    lax.fori_loop(0, levels, level, 0)

    def settle(l, carry):
        for f in range(4):
            leave(f, l).wait()
        return carry

    lax.fori_loop(0, levels, settle, 0)


def increments_of(state, level_courant, partner, geo, ends):
    fields, levels, height, width = state.shape
    nj = lax.axis_size("lon")
    vmem = pl.BlockSpec(memory_space=pltpu.VMEM)
    smem = pl.BlockSpec(memory_space=pltpu.SMEM)
    dma = pltpu.SemaphoreType.DMA
    f32 = jnp.float32
    ccol = jnp.broadcast_to(level_courant[:, None], (levels, INNER))
    clane = jnp.broadcast_to(jnp.pad(level_courant, (0, INNER - levels))[None], (8, INNER))
    meet = jnp.broadcast_to(partner.astype(f32)[None], (8, width))
    return pl.pallas_call(
        step_kernel,
        out_shape=jax.ShapeDtypeStruct((fields * levels, height, width), f32),
        in_specs=[smem, smem, vmem, vmem, vmem, vmem, vmem],
        out_specs=pl.BlockSpec(memory_space=pl.ANY),
        scratch_shapes=[
            pltpu.VMEM((fields * levels, height, width), f32),
            dma((fields * levels,)),
            pltpu.VMEM((2, 48, width), f32),
            pltpu.VMEM((2, height, INNER), f32),
            pltpu.VMEM((2, 48, width), f32),
            pltpu.VMEM((2, height, INNER), f32),
            pltpu.VMEM((nj, 48, width), f32),
            pltpu.VMEM((2, 24, width), f32),
            pltpu.VMEM((2, height, INNER), f32),
            pltpu.VMEM((6, height, INNER), f32),
            pltpu.VMEM((height + 16, width), f32),
            pltpu.VMEM((height + 16, width), f32),
            pltpu.VMEM((height + 16, width), f32),
            dma((2,)), dma((2,)), dma((2,)), dma((2,)), dma((nj,)), dma((nj,)),
        ],
        compiler_params=pltpu.CompilerParams(
            collective_id=0, has_side_effects=True, vmem_limit_bytes=58 * 1024 * 1024
        ),
        name="step",
    )(level_courant, ends, state, geo, ccol, clane, meet)


def real_forward(values):
    n = len(values)
    if n == 1:
        return [(values[0], None)]
    if n == 2:
        return [(values[0] + values[1], None), (values[0] - values[1], None)]
    even = real_forward(values[0::2])
    odd = real_forward(values[1::2])
    half = n // 2
    out = [None] * (half + 1)
    for k in range(half // 2 + 1):
        er, ei = even[k]
        orr, oi = odd[k]
        if k == 0:
            out[0] = (er + orr, None)
            out[half] = (er - orr, None)
            continue
        c, s = math.cos(2 * math.pi * k / n), math.sin(2 * math.pi * k / n)
        if k == half // 2:
            out[k] = (er, -orr)
            continue
        if oi is None:
            tr, ti = c * orr, -s * orr
        else:
            tr, ti = c * orr + s * oi, c * oi - s * orr
        eii = 0.0 if ei is None else ei
        out[k] = (er + tr, eii + ti)
        out[half - k] = (er - tr, ti - eii)
    return out


def real_backward(spec):
    n = 2 * (len(spec) - 1)
    if n == 2:
        return [spec[0][0] + spec[1][0], spec[0][0] - spec[1][0]]
    half = n // 2
    even, odd = [], []
    for k in range(half // 2 + 1):
        xr, xi = spec[k]
        yr, yi = spec[half - k]
        if k == 0:
            even.append((xr + yr, None))
            odd.append((xr - yr, None))
            continue
        if k == half // 2:
            even.append((2.0 * xr, None))
            odd.append((-2.0 * xi, None))
            continue
        c, s = math.cos(2 * math.pi * k / n), math.sin(2 * math.pi * k / n)
        dr, di = xr - yr, xi + yi
        even.append((xr + yr, xi - yi))
        odd.append((c * dr - s * di, c * di + s * dr))
    out = [None] * n
    out[0::2] = real_backward(even)
    out[1::2] = real_backward(odd)
    return out


def split(x):
    high = x.astype(jnp.bfloat16)
    return high, (x - high.astype(jnp.float32)).astype(jnp.bfloat16)


def dot3(x, w_ref):
    high, low = split(x)
    dot = functools.partial(jnp.dot, preferred_element_type=jnp.float32)
    return dot(high, w_ref[0]) + (dot(low, w_ref[0]) + dot(high, w_ref[1]))


def circle_kernel(upd, parts, inc_ref, damp_ref, twid_ref, fwd_ref, bwd_ref, out_ref, recv, done, spec, send1, recv1, send2, recv2):
    a, j = lax.axis_index("lat"), lax.axis_index("lon")
    na, nj = lax.axis_size("lat"), lax.axis_size("lon")
    quarter = na // 4
    low = a < na // 2
    active = jnp.logical_or(a < quarter, a >= na - quarter)
    mirror = jnp.where(low, 2 * quarter - 1 - a, 2 * na - 2 * quarter - 1 - a)
    source_lat = jnp.where(active, a, mirror)
    helper_lat = jnp.where(active, mirror, a)
    mine = jnp.where(active, j, nj + j)
    count = 2 * nj
    part_rows = recv.shape[2]
    width = recv.shape[3]

    def place(d):
        return (jnp.where(d < nj, source_lat, helper_lat), lax.rem(d, nj))

    def unit(ref, d, c):
        u = d * upd + c
        r = pl.multiple_of(lax.rem(u, parts) * part_rows, 8)
        return ref.at[u // parts, pl.ds(r, part_rows), :]

    barrier = pltpu.get_barrier_semaphore()

    def greet(t, carry):
        pl.semaphore_signal(barrier, inc=1, device_id=place(lax.rem(mine + t, count)), device_id_type=MESH)
        return carry

    lax.fori_loop(1, count, greet, 0)
    pl.semaphore_wait(barrier, count - 1)

    def out_copy(c, t):
        d = lax.rem(mine + t, count)
        return pltpu.make_async_remote_copy(
            unit(inc_ref, d, c), recv.at[c, j], send1.at[c, t], recv1.at[c, j],
            device_id=place(d), device_id_type=MESH)

    def out_own(c):
        return pltpu.make_async_copy(unit(inc_ref, mine, c), recv.at[c, j], recv1.at[c, j])

    def in_wait(c, s):
        return pltpu.make_async_remote_copy(
            unit(inc_ref, mine, c), recv.at[c, s], send1.at[c, 0], recv1.at[c, s],
            device_id=(source_lat, s), device_id_type=MESH)

    def back_copy(c, s):
        return pltpu.make_async_remote_copy(
            done.at[c, s], unit(out_ref, mine, c), send2.at[c, s], recv2.at[c, mine],
            device_id=(source_lat, s), device_id_type=MESH)

    def back_own(c):
        return pltpu.make_async_copy(done.at[c, j], unit(out_ref, mine, c), recv2.at[c, mine])

    def back_wait(c, d):
        return pltpu.make_async_remote_copy(
            done.at[c, j], unit(out_ref, d, c), send2.at[c, j], recv2.at[c, d],
            device_id=place(d), device_id_type=MESH)

    @pl.when(active)
    def _():
        def launch(c, carry):
            lax.fori_loop(1, count, lambda t, k: (out_copy(c, t).start(), k)[1], 0)
            out_own(c).start()
            return carry

        lax.fori_loop(0, upd, launch, 0)

    tiles = part_rows // 8
    per = width // INNER

    def handle(c, carry):
        def arrive(t, k):
            in_wait(c, lax.rem(j + t, nj)).wait_recv()
            return k

        lax.fori_loop(1, nj, arrive, 0)

        @pl.when(active)
        def _():
            out_own(c).wait()

        @pl.when(jnp.logical_not(active))
        def _():
            in_wait(c, j).wait_recv()

        def analyse(i, k):
            r = pl.ds(pl.multiple_of(i * 8, 8), 8)
            values = [
                recv[c, p // per, r, (p % per) * INNER : (p % per + 1) * INNER] for p in range(OUTER)
            ]
            for q, (re, im) in enumerate(real_forward(values)):
                cos, sin = twid_ref[0, q : q + 1, :], twid_ref[1, q : q + 1, :]
                if im is None:
                    spec[q, r, :INNER] = re * cos
                    spec[q, r, INNER:] = -re * sin
                else:
                    spec[q, r, :INNER] = re * cos + im * sin
                    spec[q, r, INNER:] = im * cos - re * sin
            return k

        lax.fori_loop(0, tiles, analyse, 0)
        h = lax.rem(mine * upd + c, parts)
        full = dot3(spec[...].reshape(HALF * part_rows, 2 * INNER), fwd_ref)
        weight = damp_ref[h].reshape(HALF * part_rows, INNER)
        full = full * jnp.concatenate([weight, weight], axis=1)
        spec[...] = dot3(full, bwd_ref).reshape(HALF, part_rows, 2 * INNER)

        def synthesise(i, k):
            r = pl.ds(pl.multiple_of(i * 8, 8), 8)
            waves = []
            for q in range(HALF):
                cos, sin = twid_ref[0, q : q + 1, :], twid_ref[1, q : q + 1, :]
                re, im = spec[q, r, :INNER], spec[q, r, INNER:]
                waves.append((re * cos - im * sin, im * cos + re * sin))
            for p, value in enumerate(real_backward(waves)):
                done[c, p // per, r, (p % per) * INNER : (p % per + 1) * INNER] = value
            return k

        lax.fori_loop(0, tiles, synthesise, 0)
        lax.fori_loop(1, nj, lambda t, k: (back_copy(c, lax.rem(j + t, nj)).start(), k)[1], 0)

        @pl.when(active)
        def _():
            back_own(c).start()

        @pl.when(jnp.logical_not(active))
        def _():
            back_copy(c, j).start()

        return carry

    lax.fori_loop(0, upd, handle, 0)

    def settle(c, carry):
        lax.fori_loop(1, nj, lambda t, k: (back_copy(c, lax.rem(j + t, nj)).wait_send(), k)[1], 0)

        @pl.when(active)
        def _():
            def finish(t, k):
                out_copy(c, t).wait_send()
                back_wait(c, lax.rem(mine + t, count)).wait_recv()
                return k

            lax.fori_loop(1, count, finish, 0)
            back_own(c).wait()

        @pl.when(jnp.logical_not(active))
        def _():
            back_copy(c, j).wait_send()

        return carry

    lax.fori_loop(0, upd, settle, 0)


def constants():
    k = np.arange(HALF)[:, None]
    q = np.arange(INNER)[None, :]
    turn = 2 * np.pi * (k * q) / (OUTER * INNER)
    twiddle = np.stack([np.cos(turn), np.sin(turn)]).astype(np.float32)
    turn = 2 * np.pi * ((q.T * q) % INNER) / INNER
    cos, sin = np.cos(turn), np.sin(turn)
    forward = np.block([[cos, -sin], [sin, cos]])

    def pair(m):
        high = m.astype(jnp.bfloat16)
        return np.stack([high, (m - high.astype(np.float64)).astype(jnp.bfloat16)])

    return jnp.asarray(twiddle), jnp.asarray(pair(forward)), jnp.asarray(pair(forward.T))


def filter_circles(inc, weights, parts, ident):
    nj = lax.axis_size("lon")
    stacks, rows, width = inc.shape
    upd = stacks * parts // (2 * nj)
    part_rows = rows // parts
    vmem = pl.BlockSpec(memory_space=pltpu.VMEM)
    hbm = pl.BlockSpec(memory_space=pl.ANY)
    dma = pltpu.SemaphoreType.DMA
    twiddle, forward, backward = constants()
    return pl.pallas_call(
        functools.partial(circle_kernel, upd, parts),
        out_shape=jax.ShapeDtypeStruct(inc.shape, jnp.float32),
        in_specs=[hbm, vmem, vmem, vmem, vmem],
        out_specs=hbm,
        scratch_shapes=[
            pltpu.VMEM((upd, nj, part_rows, width), jnp.float32),
            pltpu.VMEM((upd, nj, part_rows, width), jnp.float32),
            pltpu.VMEM((HALF, part_rows, 2 * INNER), jnp.float32),
            dma((upd, 2 * nj)),
            dma((upd, nj)),
            dma((upd, nj)),
            dma((upd, 2 * nj)),
        ],
        compiler_params=pltpu.CompilerParams(
            collective_id=ident, has_side_effects=True, vmem_limit_bytes=58 * 1024 * 1024
        ),
        name=f"circles{rows}",
    )(inc, weights, twiddle, forward, backward)


def finish_kernel(mover_ref, mask_ref, packed_ref, inc_ref, state_ref, out_ref):
    width = state_ref.shape[2]
    take = wide(mask_ref[...], width) > 0.5
    for f in range(state_ref.shape[0]):
        x = packed_ref[f]
        high = x.astype(jnp.bfloat16)
        rest = x - high.astype(jnp.float32)
        middle = rest.astype(jnp.bfloat16)
        low = (rest - middle.astype(jnp.float32)).astype(jnp.bfloat16)
        dot = functools.partial(jnp.dot, mover_ref[...], preferred_element_type=jnp.float32)
        smooth = (dot(high) + dot(middle)) + dot(low)
        out_ref[f] = state_ref[f] + jnp.where(take, smooth, inc_ref[f])


def finish(mover, mask, packed, inc, state):
    stacks, rows, width = inc.shape
    kept = packed.shape[1]
    group = 4
    whole = lambda *shape: pl.BlockSpec(shape, lambda i: (0, 0))
    block = lambda height: pl.BlockSpec((group, height, width), lambda i: (i, 0, 0))
    return pl.pallas_call(
        finish_kernel,
        grid=(stacks // group,),
        out_shape=jax.ShapeDtypeStruct(inc.shape, jnp.float32),
        in_specs=[whole(rows, kept), whole(rows, INNER), block(kept), block(rows), block(rows)],
        out_specs=block(rows),
        compiler_params=pltpu.CompilerParams(vmem_limit_bytes=40 * 1024 * 1024),
        name=f"finish{kept}",
    )(mover, mask, packed, inc, state)


def per_device(state, level_courant, damp_table, row_flag, row_table, partner):
    fields_n, levels_n, rows_n, cols_n = state.shape
    na = lax.axis_size("lat")
    a = lax.axis_index("lat")
    whole_rows = rows_n * na

    def geometry(row_pos):
        latitude = -jnp.pi / 2 + jnp.pi * (row_pos.astype(jnp.float32) + 0.5) / whole_rows
        return jnp.cos(latitude), jnp.sin(latitude)

    first_row = a * rows_n
    cos1, sin1 = geometry(first_row + jnp.arange(rows_n, dtype=jnp.int32))
    metric1 = 1.0 / jnp.maximum(cos1, cos_floor)
    geo = jnp.broadcast_to(jnp.stack([cos1, sin1, metric1])[:, :, None], (3, rows_n, INNER))
    cos_s, sin_s = geometry(first_row - 1)
    cos_n, sin_n = geometry(first_row + rows_n)
    south = a == 0
    ends = jnp.stack([
        cos_s, sin_s, cos_n, sin_n, jnp.where(south, cos1[0], cos1[-1]), jnp.where(south, sin1[0], sin1[-1])
    ])
    inc = increments_of(state, level_courant, partner, geo, ends)

    quarter = na // 4
    pairs = [(i, 2 * quarter - 1 - i if i < na // 2 else 2 * na - 2 * quarter - 1 - i) for i in range(na)]
    active = (a < quarter) | (a >= na - quarter)
    codes = jnp.stack([row_flag, row_table])
    codes = jnp.where(active, codes, lax.ppermute(codes, "lat", pairs))
    flagged, table = codes[0] == 1, codes[1]
    bands = lax.all_gather(row_flag, "lat")
    fullest = jnp.max(jnp.sum((bands == 1).astype(jnp.int32), axis=1))
    count = damp_table.shape[0]
    length = OUTER * INNER
    half = INNER // 2
    exact = lax.Precision.HIGHEST
    lower = jnp.concatenate([jnp.ones((count, 1), jnp.float32), damp_table[:, :-1]], axis=1)
    lower = jnp.transpose(lower.reshape(count, half, OUTER)[:, :, :HALF], (0, 2, 1))
    turned = damp_table.reshape(count, half, OUTER)[:, :, OUTER - HALF :]
    turn_m = jnp.asarray(np.eye(half, dtype=np.float32)[::-1].copy())
    turn_k = jnp.asarray(np.eye(HALF, dtype=np.float32)[::-1].copy())
    upper = jnp.einsum("tmj,jk,mn->tkn", turned, turn_k, turn_m, precision=exact)
    grid = jnp.concatenate([lower, upper], axis=2) * (1.0 / length)
    pick = (table[:, None] == jnp.arange(count, dtype=jnp.int32)[None, :]).astype(jnp.float32)
    rank = jnp.cumsum(flagged.astype(jnp.int32)) - 1
    spots = jnp.arange(rows_n, dtype=jnp.int32)
    packing = ((rank[None, :] == spots[:, None]) & flagged[None, :]).astype(jnp.float32)
    fewest = max(1, lax.axis_size("lon") * 2 // (fields_n * levels_n))
    unit = 8 * fewest
    sizes = [rows_n * 11 // 14 // unit * unit, rows_n * 12 // 14 // unit * unit, rows_n]

    def smoothed(ident, kept, inc):
        parts = fewest if kept % 16 else 2
        mover = packing[:kept]
        choice = jnp.dot(mover, pick, precision=exact)
        weights = jnp.einsum(
            "hrt,tkm->hkrm", choice.reshape(parts, kept // parts, count), grid, precision=exact
        )
        packed = jnp.einsum("kr,frw->fkw", mover, inc, precision=exact)
        packed = filter_circles(packed, weights, parts, ident)
        return finish(mover.T.astype(jnp.bfloat16), mask, packed, inc, state.reshape(inc.shape))

    chosen = (active & (row_flag == 1)).astype(jnp.float32)
    mask = jnp.broadcast_to(chosen[:, None], (rows_n, INNER))
    branch = sum((fullest > size).astype(jnp.int32) for size in sizes[:-1])
    result = lax.switch(
        branch, [functools.partial(smoothed, 1 + n, size) for n, size in enumerate(sizes)], inc
    )
    return result.reshape(state.shape)


def solution(mesh):
    placed = (P(None, None, "lat", "lon"), P(), P(), P("lat"), P("lat"), P("lon"))
    return jax.shard_map(
        per_device,
        mesh=mesh,
        in_specs=placed,
        out_specs=P(None, None, "lat", "lon"),
        check_vma=False,
    )
```
